256 devices in a mesh: dp: 32 (over x, y, core), expert: 8 (over z).
Axes of the slice: x: 4, y: 4, z: 8, core: 2. Of those that a mesh axis runs over, the one named last changes fastest.
Arguments:
- tokens: bfloat16 [32768, 6144], P(('dp', 'expert')), may hold values from -6 to 6
- routes: int32 [32768, 2], P('dp'), may hold values from 0 to 7, all different within a row; in each aligned block of 128 rows (0 to 127, 128 to 255, ...) at most 48 rows name the same one
- lengths: int32 [4096], P('dp'), may hold values from 1 to 8, 16384 in all
- hidden_grad: bfloat16 [32, 8, 8, 48, 8192], P('dp', 'expert'), may hold values from -6 to 6
- proj_in: bfloat16 [8, 6144, 64], P('expert'), may hold values from -0.078125 to 0.078125
- proj_out: bfloat16 [8, 8192, 128], P('expert'), may hold values from -0.0625 to 0.0625
- leaf_mix: bfloat16 [128, 128], replicated, may hold values from -1 to 1
- merge_mix: bfloat16 [128, 256], replicated, may hold values from -0.75 to 0.75
Outputs:
- sketch: bfloat16 [8, 128, 8192], P('expert', None, 'dp')
The draws below stay inside these ranges and needn't reach their ends.
Inputs may be any that keep to these rules, and one draw needn't show every extreme that they name: `routes`: within the 128 tokens of one device no expert is named more than 48 times; some device names some expert exactly 48 times. A token's 2 experts differ.
All inputs are finite; a program needn't handle non-finite values. No bound on the sum of `lengths` on one device may be relied on, other than what follows from the above.
Results may differ from the reference program's by a relative error of at most 0.015.
Values may be sent and summed in bfloat16 or wider, within the bound.
A program may use at most 64 MiB of HBM per device.

```python
import math
import jax
import jax.numpy as jnp
import numpy as np
from jax import lax

D = 6144
FF = 8192
KIN = 64
KOUT = 128
RANK = 128
TOPK = 2
SEQ_LEN = 8
SEQ_DEV = 16
EXPERTS = 8
KDIM = 8192
TOK_DEV = 128
MOST = 48
SEQ_GROUP = 128
SEQUENCES = 4096
TOKENS = 32768
LEVELS = 5
N_DP = 32
N_EXPERT = 8


def levels(stream_key, shape, cuts, low, top_value):
    gain, own = 1.0, jax.random.fold_in(stream_key, 6)
    for dim, parts in cuts:
        heights = jnp.exp(jax.random.uniform(jax.random.fold_in(own, dim), (parts,), jnp.float32, low / len(cuts), top_value / len(cuts)))
        gain = gain * jnp.repeat(heights, shape[dim] // parts).reshape([-1 if axis == dim else 1 for axis in range(len(shape))])
    return gain


def split_up(number_of, total, reach, skew):
    loads = [(1 << 20) // math.isqrt(grade ** skew) + 1 for grade in range(2, number_of + 1)]
    rest, given = total - reach - (number_of - 1), [1] * (number_of - 1)
    while rest > 0:
        movable = [i for i in range(number_of - 1) if given[i] < reach]
        whole, budget = sum([loads[i] for i in movable]), rest
        for i in movable:
            addition = min(reach - given[i], max(1, budget * loads[i] // whole), rest)
            given[i] = given[i] + addition
            rest = rest - addition
    return np.array([reach] + given)


def ragged(stream_key, count, total, most, slope):
    if count == 2:
        one = jax.random.randint(stream_key, (), max(1, total - most), min(most, total - 1) + 1)
        return jnp.stack([one, total - one])
    sizes = jnp.asarray(split_up(count, total, most, slope), jnp.int32)
    pairs = (count - 1) // 2
    giver, taker = sizes[1:1 + 2 * pairs:2], sizes[2:2 + 2 * pairs:2]
    margin = jnp.minimum(giver - 1, most - taker)
    passed = jax.random.randint(jax.random.fold_in(stream_key, 1), (pairs,), 0, 1 << 20) % (margin + 1)
    sizes = sizes.at[1:1 + 2 * pairs:2].set(giver - passed).at[2:2 + 2 * pairs:2].set(taker + passed)
    return sizes[jax.random.permutation(jax.random.fold_in(stream_key, 2), count)]


def deal_out(stream_key, own, number, rows, count, top, reach, skew):
    order = jax.random.permutation(stream_key, count)
    packed, usual = load_shares(count, rows * top, reach, skew, True), load_shares(count, rows * top, reach, skew, False)
    places = jnp.arange(count)

    def named(sizes, offset_by):
        used = int((sizes > 0).sum())
        fixed = max(1, used // 4)
        passed = fixed + (places - fixed + offset_by * (used - fixed)) % max(1, count - fixed)
        return jnp.zeros((count,), jnp.int32).at[order[jnp.where(places < fixed, places, passed)]].set(jnp.asarray(sizes, jnp.int32))

    sizes = jnp.where(number % 4 == 0, named(packed, number // 4), named(usual, number - number // 4 - 1))
    mixed = jax.random.permutation(jax.random.fold_in(own, 3), count)
    giver, receiver = mixed[0:count // 2 * 2:2], mixed[1:count // 2 * 2:2]
    margin = jnp.minimum(sizes[giver] - 1, reach - sizes[receiver]) // 2
    margin = jnp.where((giver == order[0]) | (receiver == order[0]) | (sizes[receiver] == 0), 0, jnp.maximum(margin, 0))
    passed = jax.random.randint(jax.random.fold_in(own, 4), (count // 2,), 0, 1 << 20) % (margin + 1)
    sizes = sizes.at[giver].add(-passed).at[receiver].add(passed)
    items = jnp.searchsorted(jnp.cumsum(sizes), jnp.arange(rows * top), side="right").astype(jnp.int32)
    grid = items.reshape(top, rows).T
    grid = grid[jax.random.permutation(jax.random.fold_in(own, 1), rows)]
    offset_by = jax.random.randint(jax.random.fold_in(own, 2), (rows, 1), 0, top)
    return jnp.take_along_axis(grid, (jnp.arange(top)[None, :] + offset_by) % top, axis=1)


def load_shares(count, total, bound, lean, full):
    weights = [(1 << 20) // math.isqrt(standing ** lean) + 1 for standing in range(1, count + 1)]
    largest = bound if full else min(bound, max(-(-total // count), total * weights[0] // sum(weights)))
    least = 1 if total - largest >= count - 1 else 0
    given, spare = [largest] + [least] * (count - 1), total - largest - least * (count - 1)
    while spare > 0:
        movable = [i for i in range(1, count) if given[i] < largest] or [i for i in range(1, count) if given[i] < bound]
        mass, remaining = sum([weights[i] for i in movable]), spare
        for i in movable:
            addition = min(bound - given[i], max(1, remaining * weights[i] // mass), spare)
            given[i] = given[i] + addition
            spare = spare - addition
    return np.array(given)


def normal_values(own_key, shape, width, reach, shards=(), kind=jnp.bfloat16):
    result = width * jax.random.normal(own_key, shape, jnp.float32)
    if shards:
        result = result * levels(own_key, shape, shards, -0.22, 0.18)
    return jnp.clip(result, -reach, reach).astype(kind)


def setup_inputs(seed: int = 0) -> dict:
    key_list = jax.random.split(jax.random.key(seed), 9)
    tokens = normal_values(key_list[0], (TOKENS, D), 1.0, 6.0, ((0, 256),))
    routes_keys = jax.random.split(jax.random.fold_in(key_list[1], 1), TOKENS // TOK_DEV)
    routes_turns = jax.random.permutation(jax.random.fold_in(key_list[1], 3), TOKENS // TOK_DEV)
    routes = jax.vmap(lambda own, number: deal_out(jax.random.fold_in(key_list[1], 2), own, number, TOK_DEV, EXPERTS, TOPK, MOST, 2))(routes_keys, routes_turns).reshape((TOKENS, TOPK))
    lengths = ragged(key_list[2], SEQUENCES, SEQ_LEN * SEQUENCES // 2, SEQ_LEN, 1).astype(jnp.int32)
    hidden_grad = normal_values(key_list[3], (N_DP, EXPERTS, N_EXPERT, MOST, FF), 1.0, 6.0, ((0, 32), (1, 8)))
    proj_in = normal_values(key_list[4], (EXPERTS, D, KIN), D ** -0.5, 0.078125, ((0, 8),))
    proj_out = normal_values(key_list[5], (EXPERTS, FF, KOUT), FF ** -0.5, 0.0625, ((0, 8),))
    leaf_mix = normal_values(key_list[6], (RANK, SEQ_GROUP), (SEQ_GROUP // 4) ** -0.5, 1.0)
    merge_mix = normal_values(key_list[7], (RANK, 2 * RANK), (RANK // 2) ** -0.5, 0.75)
    return dict(tokens=tokens, routes=routes, lengths=lengths, hidden_grad=hidden_grad, proj_in=proj_in, proj_out=proj_out, leaf_mix=leaf_mix, merge_mix=merge_mix)


epsilon = 1e-6


def slot_table(block_routes, experts_count, capacity):
    flat = block_routes.reshape(-1).astype(jnp.int32)
    labels = jnp.arange(experts_count, dtype=jnp.int32)
    onehot = (flat[:, None] == labels[None, :]).astype(jnp.int32)
    before = jnp.cumsum(onehot, axis=0) - onehot
    position = jnp.sum(before * onehot, axis=1).astype(jnp.int32)
    owner = (jnp.arange(flat.shape[0], dtype=jnp.int32) // block_routes.shape[1]).astype(jnp.int32)
    empty = jnp.full((experts_count, capacity), -1, jnp.int32)
    return empty.at[flat, position].set(owner)


def slot_weights(table_src, lengths_group, seq_len, seq_dev, seq_group):
    source = jnp.arange(table_src.shape[0], dtype=jnp.int32)[:, None]
    clipped = jnp.maximum(table_src, 0)
    sequence = (source * seq_dev + clipped // seq_len).astype(jnp.int32)
    live_slot = (table_src >= 0) & (clipped % seq_len < lengths_group[sequence])
    sequence = sequence.reshape(-1)
    live_slot = live_slot.reshape(-1)
    labels = jnp.arange(seq_group, dtype=jnp.int32)
    return ((sequence[None, :] == labels[:, None]) & live_slot[None, :]).astype(jnp.bfloat16)


def shrink_rows(mixed):
    energy = jnp.sum(mixed * mixed, axis=-1)
    threshold = jnp.mean(energy, axis=-1, keepdims=True)
    factor = energy / (energy + threshold + epsilon)
    return (mixed * factor[..., None]).astype(jnp.bfloat16)


def reference(tokens, routes, lengths, hidden_grad, proj_in, proj_out, leaf_mix, merge_mix):
    tokens_grouped = tokens.reshape(N_DP, N_EXPERT, TOK_DEV, D)
    routes_grouped = routes.reshape(N_DP, N_EXPERT, TOK_DEV, TOPK)
    lengths_grouped = lengths.reshape(N_DP, SEQ_GROUP)

    def one_group(inputs):
        token_block, route_block, length_block, grad_block = inputs
        tables = jnp.stack([slot_table(route_block[source_index], EXPERTS, MOST) for source_index in range(N_EXPERT)])
        leaves = []
        for expert in range(EXPERTS):
            table_src = tables[:, expert]
            source = jnp.arange(N_EXPERT, dtype=jnp.int32)[:, None]
            gathered = token_block[source, jnp.maximum(table_src, 0)]
            feature_proj = jnp.dot(gathered.reshape(-1, D), proj_in[expert], preferred_element_type=jnp.float32)
            grad_proj = jnp.dot(grad_block[expert].reshape(-1, FF), proj_out[expert], preferred_element_type=jnp.float32)
            outer = (feature_proj[:, :, None] * grad_proj[:, None, :]).reshape(-1, KDIM).astype(jnp.bfloat16)
            weights = slot_weights(table_src, length_block, SEQ_LEN, SEQ_DEV, SEQ_GROUP)
            per_seq = jnp.dot(weights, outer, preferred_element_type=jnp.float32).astype(jnp.bfloat16)
            leaves.append(shrink_rows(jnp.dot(leaf_mix, per_seq, preferred_element_type=jnp.float32)))
        return jnp.stack(leaves)

    leaves = lax.map(one_group, (tokens_grouped, routes_grouped, lengths_grouped, hidden_grad))
    mixing = merge_mix.astype(jnp.float32)
    results = []
    for expert in range(EXPERTS):
        current = leaves[:, expert]
        for level_number in range(LEVELS):
            node_count = current.shape[0]
            paired = current.reshape(node_count // 2, 2 * RANK, KDIM).astype(jnp.float32)
            mixed = jnp.einsum('rq,mqk->mrk', mixing, paired)
            current = shrink_rows(mixed)
        results.append(current[0])
    return jnp.stack(results)
```

```python
import jax
import jax.numpy as jnp
from jax import lax
from jax.sharding import PartitionSpec as P

SEQ_LEN = 8
EPSILON = 1e-06


def slots(own, expert, seq_len, capacity):
    match = own == expert
    count = own.shape[-1]
    row = lax.broadcasted_iota(jnp.int32, (count, count), 0)
    col = lax.broadcasted_iota(jnp.int32, (count, count), 1)
    earlier = (row < col).astype(jnp.bfloat16)
    before = jnp.dot(match.astype(jnp.bfloat16), earlier, preferred_element_type=jnp.float32)
    place = jnp.where(match, before, -1.0).astype(jnp.int32)
    place = place.reshape(own.shape[0], count // 2, 2)
    cell = jnp.arange(capacity, dtype=jnp.int32)
    return jnp.any(place[:, None] == cell[None, :, None, None], axis=-1)


def factors(energy):
    threshold = jnp.mean(energy, axis=-1, keepdims=True)
    return energy / (energy + threshold + EPSILON)


def shards(tokens, routes, lengths, hidden_grad, proj_in, proj_out, leaf_mix, merge_mix):
    n_expert = lax.axis_size("expert")
    n_dp = lax.axis_size("dp")
    expert_id = lax.axis_index("expert")
    dp_index = lax.axis_index("dp")
    tok_dev, width = tokens.shape
    capacity = hidden_grad.shape[3]
    kin = proj_in.shape[2]
    kout = proj_out.shape[2]
    seq_group = lengths.shape[0]
    seq_dev = seq_group // n_expert

    bands, strips = kin // 8, n_dp // (kin // 8)
    strip = width // strips
    piece = lax.dynamic_slice(
        proj_in[0].T, (dp_index // strips * 8, dp_index % strips * strip), (8, strip)
    )
    every = lax.all_gather(piece, ("dp", "expert")).reshape(bands, strips, n_expert * 8, strip)

    grad_rows = hidden_grad[0, 0].reshape(-1, hidden_grad.shape[4])
    grad_proj = jnp.dot(grad_rows, proj_out[0], preferred_element_type=jnp.float32)

    group_routes = routes.reshape(n_expert, -1)
    held = slots(group_routes, expert_id, SEQ_LEN, capacity)
    token_seq = jnp.arange(tok_dev, dtype=jnp.int32) // SEQ_LEN
    seq = jnp.sum(jnp.where(held, token_seq, 0), axis=-1)
    seq = seq + jnp.arange(n_expert, dtype=jnp.int32)[:, None] * seq_dev
    slot_count = n_expert * capacity
    code = seq.reshape(slot_count // kout, kout).astype(jnp.bfloat16)
    packed = jnp.concatenate([grad_proj.astype(jnp.bfloat16), code], axis=0)
    packed = lax.all_gather(packed, "dp")
    grads = packed[:, :slot_count]
    codes = packed[:, slot_count:].reshape(n_dp, slot_count).astype(jnp.int32)

    feature = jnp.zeros((tok_dev, bands * n_expert * 8), jnp.float32)
    for s in range(strips):
        block = every[:, s].reshape(bands * n_expert * 8, strip)
        feature += lax.dot_general(
            tokens[:, s * strip : (s + 1) * strip],
            block,
            (((1,), (1,)), ((), ())),
            preferred_element_type=jnp.float32,
        )
    feature = feature.astype(jnp.bfloat16).reshape(tok_dev, bands, n_expert, 8)
    feature = feature.transpose(2, 0, 1, 3).reshape(n_expert, tok_dev, kin)
    own_routes = lax.dynamic_slice_in_dim(group_routes, expert_id, 1, 0)
    own_lengths = lax.dynamic_slice_in_dim(lengths, expert_id * seq_dev, seq_dev, 0)
    place = jnp.arange(tok_dev, dtype=jnp.int32)
    live = (place.reshape(seq_dev, SEQ_LEN) % SEQ_LEN < own_lengths[:, None]).reshape(tok_dev)
    labels = jnp.arange(n_expert, dtype=jnp.int32)
    chosen = slots(jnp.broadcast_to(own_routes, (n_expert, own_routes.shape[1])), labels[:, None], SEQ_LEN, capacity)
    chosen = (chosen & live).astype(jnp.bfloat16)
    sent = jnp.einsum("ect,etk->eck", chosen, feature, preferred_element_type=jnp.float32).astype(jnp.bfloat16)
    got = lax.all_to_all(sent, "expert", split_axis=0, concat_axis=0, tiled=True)
    columns = got.reshape(slot_count, kin).T.reshape(n_dp, kin // n_dp, slot_count)
    mine = lax.all_to_all(columns, "dp", split_axis=0, concat_axis=0, tiled=True)

    belongs = codes[:, None, :] == jnp.arange(seq_group, dtype=jnp.int32)[None, :, None]
    spread = jnp.where(belongs[:, None], mine[:, :, None, :], jnp.zeros((), jnp.bfloat16))
    per_seq = jnp.einsum("gisc,gck->gsik", spread, grads, preferred_element_type=jnp.float32)
    per_seq = per_seq.astype(jnp.bfloat16).reshape(n_dp, seq_group, -1)
    mixed = jnp.einsum("rs,gsk->grk", leaf_mix, per_seq, preferred_element_type=jnp.float32)
    while True:
        energy = lax.psum(jnp.sum(mixed * mixed, axis=-1), "dp")
        current = (mixed * factors(energy)[..., None]).astype(jnp.bfloat16)
        if current.shape[0] == 1:
            return current
        stacked = current.reshape(current.shape[0] // 2, -1, current.shape[2])
        mixed = jnp.einsum("rq,mqk->mrk", merge_mix, stacked, preferred_element_type=jnp.float32)


def solution(mesh):
    in_specs = (
        P(("dp", "expert"), None),
        P("dp", None),
        P("dp"),
        P("dp", "expert", None, None, None),
        P("expert", None, None),
        P("expert", None, None),
        P(),
        P(),
    )
    out_specs = P("expert", None, "dp")
    return jax.shard_map(shards, mesh=mesh, in_specs=in_specs, out_specs=out_specs, check_vma=False)
```

```python
import functools

import jax
import jax.numpy as jnp
from jax import lax
from jax.experimental import pallas as pl
from jax.experimental.pallas import tpu as pltpu
from jax.sharding import PartitionSpec as P

SEQ_LEN = 8
EPSILON = 1e-06
MESH = pl.DeviceIdType.MESH
NX, NY, NC = 4, 4, 2
SIDE = NY * NC
F32 = jnp.float32
BF16 = jnp.bfloat16


def slots(own, expert, seq_len, capacity):
    match = own == expert
    count = own.shape[-1]
    row = lax.broadcasted_iota(jnp.int32, (count, count), 0)
    col = lax.broadcasted_iota(jnp.int32, (count, count), 1)
    earlier = (row < col).astype(BF16)
    before = jnp.dot(match.astype(BF16), earlier, preferred_element_type=F32)
    place = jnp.where(match, before, -1.0).astype(jnp.int32)
    place = place.reshape(own.shape[0], count // 2, 2)
    cell = jnp.arange(capacity, dtype=jnp.int32)
    return jnp.any(place[:, None] == cell[None, :, None, None], axis=-1)


def factors(energy):
    threshold = jnp.mean(energy, axis=-1, keepdims=True)
    return energy / (energy + threshold + EPSILON)


def remote(src, dst, send, recv, dp, expert):
    return pltpu.make_async_remote_copy(
        src_ref=src, dst_ref=dst, send_sem=send, recv_sem=recv,
        device_id={"dp": dp, "expert": expert}, device_id_type=MESH,
    )


def as_rows(column_sums, count):
    lane = lax.broadcasted_iota(jnp.int32, (128, 128), 1)
    square = jnp.zeros((128, 128), F32)
    for n, sums in enumerate(column_sums):
        square = jnp.where(lane == n, sums, square)
    return square.T[:count]


def tree_kernel(
    feats, grads, codes, leaf_mix, merge_mix, out, nodes, nodes_b, lines, corner, corner_b,
    side, rows, side_send, side_recv, row_send, row_recv, line_send, line_recv,
):
    me, expert = lax.axis_index("dp"), lax.axis_index("expert")
    x = me // SIDE
    barrier = pltpu.get_barrier_semaphore()
    peers = [me ^ k for k in range(1, SIDE)] + [me ^ (SIDE * k) for k in range(1, NX)]
    for peer in peers:
        pl.semaphore_signal(barrier, inc=1, device_id={"dp": peer, "expert": expert}, device_id_type=MESH)
    pl.semaphore_wait(barrier, len(peers))

    def side_sum(rnd, energy):
        side[rnd, 0] = energy
        copies = [
            remote(side.at[rnd, 0], side.at[rnd, k], side_send.at[rnd, k], side_recv.at[rnd, k], me ^ k, expert)
            for k in range(1, SIDE)
        ]
        for c in copies:
            c.start()
        for c in copies:
            c.wait()
        return jnp.sum(side[rnd], axis=0)

    def row_share(rnd, energy):
        rows[rnd, 0] = energy
        copies = [
            remote(rows.at[rnd, 0], rows.at[rnd, k], row_send.at[rnd, k], row_recv.at[rnd, k], me ^ (SIDE * k), expert)
            for k in range(1, NX)
        ]
        for c in copies:
            c.start()
        for c in copies:
            c.wait()

    groups, each, slot_count = feats.shape
    seqs = leaf_mix.shape[0]
    label = lax.broadcasted_iota(jnp.int32, (seqs, slot_count), 0)
    sums = []
    for g in range(groups):
        belongs = codes[g : g + 1] == label
        spread = jnp.concatenate(
            [jnp.where(belongs, feats[g, i : i + 1], 0.0).astype(BF16) for i in range(each)], axis=0
        )
        per_seq = jnp.dot(spread, grads[g], preferred_element_type=F32).astype(BF16)
        total = jnp.zeros((seqs, 128), F32)
        for h in range(each // 2):
            pair = jnp.concatenate([per_seq[(2 * h + b) * seqs : (2 * h + b + 1) * seqs] for b in range(2)], axis=1)
            mixed = jnp.dot(leaf_mix[...], pair, preferred_element_type=F32)
            nodes[g * 128 : (g + 1) * 128, h * 256 : (h + 1) * 256] = mixed.astype(BF16)
            total += mixed[:, :128] * mixed[:, :128] + mixed[:, 128:] * mixed[:, 128:]
        sums.append(jnp.sum(total, axis=1, keepdims=True))
    energy = side_sum(0, as_rows(sums, 8))

    source, target, count = nodes, nodes_b, groups
    for level in range(3):
        factor = factors(energy)
        sums = []
        for m in range(count // 2):
            weight = jnp.concatenate([factor[2 * m : 2 * m + 1], factor[2 * m + 1 : 2 * m + 2]], axis=1)
            weight = (merge_mix[...].astype(F32) * weight).astype(BF16)
            total = jnp.zeros((128, 128), F32)
            for h in range(NX):
                columns = slice(h * 256, (h + 1) * 256)
                mixed = jnp.dot(weight, source[m * 256 : (m + 1) * 256, columns], preferred_element_type=F32)
                target[m * 128 : (m + 1) * 128, columns] = mixed.astype(BF16)
                total += mixed[:, :128] * mixed[:, :128] + mixed[:, 128:] * mixed[:, 128:]
            sums.append(jnp.sum(total, axis=1, keepdims=True))
        source, target, count = target, source, count // 2
        if level == 2:
            for h in range(NX):
                lines[h] = source[0:128, h * 256 : (h + 1) * 256]
            shares = []
            for k in range(1, NX):
                shares.append(remote(
                    lines.at[x ^ k], corner.at[k], line_send.at[k], line_recv.at[k], me ^ (SIDE * k), expert
                ))
            for c in shares:
                c.start()
            corner[0] = lines[x]
        energy = side_sum(1 + level, as_rows(sums, 8))

    row_share(0, energy)
    for c in shares:
        c.wait()
    sums = []
    for m in range(2):
        low, high = x ^ (2 * m), x ^ (2 * m + 1)
        weight = [factors(rows[0, k][0:1]) for k in (low, high)]
        weight = (merge_mix[...].astype(F32) * jnp.concatenate(weight, axis=1)).astype(BF16)
        stacked = jnp.concatenate([corner[low], corner[high]], axis=0)
        mixed = jnp.dot(weight, stacked, preferred_element_type=F32)
        corner_b[m * 128 : (m + 1) * 128] = mixed.astype(BF16)
        sums.append(jnp.sum(mixed * mixed, axis=1, keepdims=True))
    row_share(1, side_sum(4, as_rows(sums, 8)))
    factor = factors(jnp.sum(rows[1], axis=0))
    weight = jnp.concatenate([factor[0:1], factor[1:2]], axis=1)
    weight = (merge_mix[...].astype(F32) * weight).astype(BF16)
    mixed = jnp.dot(weight, corner_b[...], preferred_element_type=F32)
    row_share(2, side_sum(5, as_rows([jnp.sum(mixed * mixed, axis=1, keepdims=True)], 8)))
    factor = factors(jnp.sum(rows[2], axis=0))
    factor = jnp.broadcast_to(factor[0:1], (128, 128)).T
    out[...] = (mixed * jnp.concatenate([factor, factor], axis=1)).astype(BF16)


def tree(feats, grads, codes, leaf_mix, merge_mix):
    groups, each, _ = feats.shape
    width = each * grads.shape[2]
    return pl.pallas_call(
        tree_kernel,
        out_shape=jax.ShapeDtypeStruct((128, 256), BF16),
        in_specs=[pl.BlockSpec(memory_space=pltpu.VMEM)] * 5,
        out_specs=pl.BlockSpec(memory_space=pltpu.VMEM),
        scratch_shapes=[
            pltpu.VMEM((groups * 128, width), BF16),
            pltpu.VMEM((groups * 64, width), BF16),
            pltpu.VMEM((NX, 128, 256), BF16),
            pltpu.VMEM((NX, 128, 256), BF16),
            pltpu.VMEM((256, 256), BF16),
            pltpu.VMEM((6, SIDE, 8, 128), F32),
            pltpu.VMEM((3, NX, 8, 128), F32),
            pltpu.SemaphoreType.DMA((6, SIDE)),
            pltpu.SemaphoreType.DMA((6, SIDE)),
            pltpu.SemaphoreType.DMA((3, NX)),
            pltpu.SemaphoreType.DMA((3, NX)),
            pltpu.SemaphoreType.DMA((NX,)),
            pltpu.SemaphoreType.DMA((NX,)),
        ],
        compiler_params=pltpu.CompilerParams(
            collective_id=0, has_side_effects=True, vmem_limit_bytes=40 << 20
        ),
    )(feats, grads, codes, leaf_mix, merge_mix)


def shards(tokens, routes, lengths, hidden_grad, proj_in, proj_out, leaf_mix, merge_mix):
    n_expert = lax.axis_size("expert")
    n_dp = lax.axis_size("dp")
    expert_id = lax.axis_index("expert")
    dp_index = lax.axis_index("dp")
    tok_dev, width = tokens.shape
    capacity = hidden_grad.shape[3]
    kin = proj_in.shape[2]
    kout = proj_out.shape[2]
    seq_group = lengths.shape[0]
    seq_dev = seq_group // n_expert

    bands, strips = kin // 8, n_dp // (kin // 8)
    strip = width // strips
    piece = lax.dynamic_slice(
        proj_in[0].T, (dp_index // strips * 8, dp_index % strips * strip), (8, strip)
    )
    every = lax.all_gather(piece, ("dp", "expert")).reshape(bands, strips, n_expert * 8, strip)

    grad_rows = hidden_grad[0, 0].reshape(-1, hidden_grad.shape[4])
    grad_proj = jnp.dot(grad_rows, proj_out[0], preferred_element_type=F32)

    group_routes = routes.reshape(n_expert, -1)
    held = slots(group_routes, expert_id, SEQ_LEN, capacity)
    token_seq = jnp.arange(tok_dev, dtype=jnp.int32) // SEQ_LEN
    seq = jnp.sum(jnp.where(held, token_seq, 0), axis=-1)
    seq = seq + jnp.arange(n_expert, dtype=jnp.int32)[:, None] * seq_dev
    slot_count = n_expert * capacity
    code = seq.reshape(slot_count // kout, kout).astype(BF16)
    packed = jnp.concatenate([grad_proj.astype(BF16), code], axis=0)
    x_groups = [[x * SIDE + k for k in range(SIDE)] for x in range(NX)]
    packed = lax.all_gather(packed, "dp", axis_index_groups=x_groups)
    grads = packed[:, :slot_count]
    codes = packed[:, slot_count:].reshape(SIDE, slot_count).astype(jnp.int32)

    feature = jnp.zeros((tok_dev, bands * n_expert * 8), F32)
    for s in range(strips):
        block = every[:, s].reshape(bands * n_expert * 8, strip)
        feature += lax.dot_general(
            tokens[:, s * strip : (s + 1) * strip],
            block,
            (((1,), (1,)), ((), ())),
            preferred_element_type=F32,
        )
    feature = feature.astype(BF16).reshape(tok_dev, bands, n_expert, 8)
    feature = feature.transpose(2, 0, 1, 3).reshape(n_expert, tok_dev, kin)
    own_routes = lax.dynamic_slice_in_dim(group_routes, expert_id, 1, 0)
    own_lengths = lax.dynamic_slice_in_dim(lengths, expert_id * seq_dev, seq_dev, 0)
    place = jnp.arange(tok_dev, dtype=jnp.int32)
    live = (place.reshape(seq_dev, SEQ_LEN) % SEQ_LEN < own_lengths[:, None]).reshape(tok_dev)
    labels = jnp.arange(n_expert, dtype=jnp.int32)
    chosen = slots(jnp.broadcast_to(own_routes, (n_expert, own_routes.shape[1])), labels[:, None], SEQ_LEN, capacity)
    chosen = (chosen & live).astype(BF16)
    sent = jnp.einsum("ect,etk->eck", chosen, feature, preferred_element_type=F32).astype(BF16)
    got = lax.all_to_all(sent, "expert", split_axis=0, concat_axis=0, tiled=True)
    columns = got.reshape(slot_count, NX, NY, NC, 2).transpose(2, 3, 1, 4, 0).reshape(SIDE, 2 * NX, slot_count)
    mine = lax.all_to_all(columns, "dp", split_axis=0, concat_axis=0, tiled=True, axis_index_groups=x_groups)
    return tree(mine.astype(F32), grads, codes, leaf_mix, merge_mix)[None]


def solution(mesh):
    in_specs = (
        P(("dp", "expert"), None),
        P("dp", None),
        P("dp"),
        P("dp", "expert", None, None, None),
        P("expert", None, None),
        P("expert", None, None),
        P(),
        P(),
    )
    out_specs = P("expert", None, "dp")
    return jax.shard_map(shards, mesh=mesh, in_specs=in_specs, out_specs=out_specs, check_vma=False)
```

```python
import jax
import jax.numpy as jnp
from jax import lax
from jax.experimental import pallas as pl
from jax.experimental.pallas import tpu as pltpu
from jax.sharding import PartitionSpec as P

SEQ_LEN = 8
EPSILON = 1e-06
MESH = pl.DeviceIdType.MESH
NX, NY, NC, NZ = 4, 4, 2, 8
SIDE = NY * NC
CHUNKS = 8
F32 = jnp.float32
BF16 = jnp.bfloat16


def factors(energy):
    threshold = jnp.mean(energy, axis=-1, keepdims=True)
    return energy / (energy + threshold + EPSILON)


def remote(src, dst, send, recv, dp, expert):
    return pltpu.make_async_remote_copy(
        src_ref=src, dst_ref=dst, send_sem=send, recv_sem=recv,
        device_id={"dp": dp, "expert": expert}, device_id_type=MESH,
    )


def as_rows(column_sums, count):
    lane = lax.broadcasted_iota(jnp.int32, (128, 128), 1)
    square = jnp.zeros((128, 128), F32)
    for n, sums in enumerate(column_sums):
        square = jnp.where(lane == n, sums, square)
    return square.T[:count]


def kernel(
    tokens, routes, lengths, hidden, proj_in, proj_out, leaf_mix, merge_mix, out,
    both, raw, weights, grad_in, grad_mix, feature, places, codes, grads, sent, got, turned, feats,
    nodes, nodes_b, lines, corner, corner_b, side, rows,
    local, token_sem, place_sem, code_send, code_recv, grad_send, grad_recv, pass_send, pass_recv,
    piece_send, piece_recv, ring_send, ring_recv, slot_send, slot_recv, feat_send, feat_recv,
    side_send, side_recv, row_send, row_recv, line_send, line_recv,
):
    me, expert = lax.axis_index("dp"), lax.axis_index("expert")
    x, y, core = me // SIDE, (me // NC) % NY, me % NC
    pair = me ^ 1
    n_expert = NZ
    tok_dev = tokens.shape[0]
    depth = tokens.shape[1] // (NX * NY)
    capacity = sent.shape[2]
    slot_count = n_expert * capacity
    half_kin = weights.shape[2] // n_expert

    spot = (x * NY + y) * depth
    load_piece = pltpu.make_async_copy(
        proj_in.at[:, pl.ds(pl.multiple_of(spot, 128), depth)], raw, local.at[0]
    )
    load_piece.start()
    own_rows = pl.ds(pl.multiple_of(core * tok_dev, tok_dev), tok_dev)
    load_tokens = pltpu.make_async_copy(tokens, both.at[own_rows], local.at[1])
    chunk = hidden.shape[1] // CHUNKS
    loads = []
    for n in range(CHUNKS):
        part = slice(n * chunk, (n + 1) * chunk)
        loads.append((
            pltpu.make_async_copy(hidden.at[:, part], grad_in.at[n], local.at[2 + 2 * n]),
            pltpu.make_async_copy(proj_out.at[part], grad_mix.at[n], local.at[3 + 2 * n]),
        ))
    for pair_of_loads in loads:
        for c in pair_of_loads:
            c.start()
    load_tokens.start()

    barrier = pltpu.get_barrier_semaphore()
    peers = [me ^ k for k in range(1, SIDE)] + [me ^ (SIDE * k) for k in range(1, NX)]
    for peer in peers:
        pl.semaphore_signal(barrier, inc=1, device_id={"dp": peer, "expert": expert}, device_id_type=MESH)
    for k in range(1, NZ):
        pl.semaphore_signal(barrier, inc=1, device_id={"dp": me, "expert": expert ^ k}, device_id_type=MESH)
    pl.semaphore_wait(barrier, len(peers) + NZ - 1)

    load_piece.wait()
    r = lax.broadcasted_iota(jnp.int32, (half_kin, 2 * half_kin), 0)
    c = lax.broadcasted_iota(jnp.int32, (half_kin, 2 * half_kin), 1)
    wanted = (r % 8) // 2 * 16 + r // 8 * 4 + core * 2 + r % 2
    pick = (wanted == c).astype(BF16)
    own_piece = weights.at[x, y, pl.ds(pl.multiple_of(expert * half_kin, half_kin), half_kin)]
    own_piece[...] = jnp.dot(pick, raw[...], preferred_element_type=F32).astype(BF16)
    pieces = [
        remote(own_piece, own_piece, piece_send.at[k], piece_recv.at[k], me, expert ^ k)
        for k in range(1, NZ)
    ]
    for c in pieces:
        c.start()
    share_tokens = remote(tokens, both.at[own_rows], token_sem.at[0], token_sem.at[1], pair, expert)
    share_tokens.start()

    r = lax.broadcasted_iota(jnp.int32, (tok_dev, tok_dev), 0)
    c = lax.broadcasted_iota(jnp.int32, (tok_dev, tok_dev), 1)
    earlier = (r < c).astype(BF16)
    seq_dev = tok_dev // SEQ_LEN
    lasting = jnp.broadcast_to(lengths[...], (8, tok_dev)).astype(F32).astype(BF16)
    owner = (r == expert * seq_dev + c // SEQ_LEN).astype(BF16)
    lasting = jnp.dot(lasting, owner, preferred_element_type=F32)
    r = lax.broadcasted_iota(jnp.int32, (8, tok_dev), 0)
    c = lax.broadcasted_iota(jnp.int32, (8, tok_dev), 1)
    live = (c % SEQ_LEN).astype(F32) < lasting

    def placed(match):
        before = jnp.dot(match.astype(F32).astype(BF16), earlier, preferred_element_type=F32)
        return jnp.where(match, before, -1.0)

    here = pl.ds(pl.multiple_of(expert * tok_dev, tok_dev), tok_dev)
    match = (routes[0:1, here] == r) | (routes[1:2, here] == r)
    places[core] = jnp.where(live, placed(match), -1.0)
    share_places = remote(places.at[core], places.at[core], place_sem.at[0], place_sem.at[1], pair, expert)
    share_places.start()
    first = jnp.concatenate([routes[0:1, j * tok_dev : (j + 1) * tok_dev] for j in range(n_expert)], axis=0)
    second = jnp.concatenate([routes[1:2, j * tok_dev : (j + 1) * tok_dev] for j in range(n_expert)], axis=0)
    place = placed((first == expert) | (second == expert))
    cell = lax.broadcasted_iota(jnp.int32, (capacity, tok_dev), 0).astype(F32)
    held = jnp.concatenate([(place[j : j + 1] == cell).astype(F32).astype(BF16) for j in range(n_expert)], axis=0)
    number = (c // SEQ_LEN).astype(F32).astype(BF16)
    code = lax.dot_general(number, held, (((1,), (1,)), ((), ())), preferred_element_type=F32)
    source = lax.broadcasted_iota(jnp.int32, (8, slot_count), 1) // capacity
    group = me % SIDE
    codes[group] = code + (source * seq_dev).astype(F32)
    share_codes = [
        remote(codes.at[group], codes.at[group], code_send.at[k], code_recv.at[k], me ^ k, expert)
        for k in range(1, SIDE)
    ]
    for c in share_codes:
        c.start()

    total = jnp.zeros((slot_count, grads.shape[2]), F32)
    for n in range(CHUNKS):
        for c in loads[n]:
            c.wait()
        total += jnp.dot(grad_in[n], grad_mix[n], preferred_element_type=F32)
    grads[group] = total.astype(BF16)

    for c in pieces:
        c.wait()
    up_x, down_x = (x + 1) % NX, (x + NX - 1) % NX
    up_y, down_y = (y + 1) % NY, (y + NY - 1) % NY
    at_x = lambda to: to * SIDE + y * NC + core
    at_y = lambda to: x * SIDE + to * NC + core
    half = weights.shape[2] // 2
    low, high = slice(0, half), slice(half, 2 * half)
    quarter = half // 2

    def along(block, n, target, up, down, own):
        there = []
        for way, to in enumerate((up, down)):
            there.append(remote(
                block(own, 0, half), block(own, 0, half), ring_send.at[n, way], ring_recv.at[n, way], target(to), expert
            ))
        for c in there:
            c.start()

        def onward():
            further = []
            for way, (to, came) in enumerate(((up, down), (down, up))):
                there[way].wait_recv()
                view = block(came, way * quarter, quarter)
                c = remote(view, view, ring_send.at[n, 2 + way], ring_recv.at[n, 2 + way], target(to), expert)
                c.start()
                further.append(c)
            return there + further

        return there, onward

    def finish(copies):
        for c in copies[:2]:
            c.wait_send()
        for c in copies[2:]:
            c.wait()

    share_grads = []
    _, onward_a = along(lambda i, s, w: weights.at[i, y, pl.ds(s, w)], 0, at_x, up_x, down_x, x)
    _, onward_b = along(lambda i, s, w: weights.at[x, i, pl.ds(half + s, w)], 1, at_y, up_y, down_y, y)
    share_grads = [
        remote(grads.at[group], grads.at[group], grad_send.at[k], grad_recv.at[k], me ^ (NC * k) if k else pair, expert)
        for k in range(NY)
    ]
    for c in share_grads:
        c.start()
    copies_a, copies_b = onward_a(), onward_b()
    finish(copies_a)
    finish(copies_b)
    _, onward_a = along(lambda i, s, w: weights.at[:, i, pl.ds(s, w)], 2, at_y, up_y, down_y, y)
    _, onward_b = along(lambda i, s, w: weights.at[i, :, pl.ds(half + s, w)], 3, at_x, up_x, down_x, x)
    pass_grads = []
    for k in range(1, NY):
        share_grads[k].wait()
        far = group ^ (NC * k)
        c = remote(grads.at[far], grads.at[far], pass_send.at[k], pass_recv.at[k], pair, expert)
        c.start()
        pass_grads.append(c)
    load_tokens.wait()
    share_tokens.wait()
    share_places.wait()
    copies_a, copies_b = onward_a(), onward_b()
    finish(copies_a)
    finish(copies_b)

    feature[...] = jnp.zeros_like(feature)
    for n in range(NX * NY):
        feature[...] += lax.dot_general(
            both[:, n * depth : (n + 1) * depth], weights[n // NY, n % NY],
            (((1,), (1,)), ((), ())), preferred_element_type=F32,
        )
    for h in range(NC):
        chosen = jnp.concatenate(
            [(places[h, e : e + 1] == cell).astype(F32).astype(BF16) for e in range(n_expert)], axis=0
        )
        slots = jnp.dot(chosen, feature[h * tok_dev : (h + 1) * tok_dev].astype(BF16), preferred_element_type=F32)
        for e in range(n_expert):
            lanes = e * half_kin // 128 * 128
            sent[e, h] = slots[e * capacity : (e + 1) * capacity, lanes : lanes + 128].astype(BF16)
    share_slots = [
        remote(sent.at[expert ^ k], got.at[expert], slot_send.at[k], slot_recv.at[k], me, expert ^ k)
        for k in range(1, NZ)
    ]
    for c in share_slots:
        c.start()
    got[expert] = sent[expert]
    for c in share_codes:
        c.wait()
    share_grads[0].wait()
    for c in pass_grads:
        c.wait()
    for c in share_slots:
        c.wait()
    r = lax.broadcasted_iota(jnp.int32, (half_kin, 128), 0)
    c = lax.broadcasted_iota(jnp.int32, (half_kin, 128), 1)
    pick = (c == expert * half_kin % 128 + r).astype(BF16)
    for h in range(NC):
        everything = jnp.concatenate([got[j, h] for j in range(n_expert)], axis=0)
        lines_of = lax.dot_general(pick, everything, (((1,), (1,)), ((), ())), preferred_element_type=F32)
        for to in range(NY):
            turned[to, h] = lines_of[to * 8 : (to + 1) * 8]
    share_feats = [
        remote(
            turned.at[y ^ k], feats.at[pl.ds(NC * y, NC)], feat_send.at[k], feat_recv.at[k], me ^ (NC * k), expert
        )
        for k in range(1, NY)
    ]
    for c in share_feats:
        c.start()
    feats[pl.ds(NC * y, NC)] = turned[y]
    for c in share_feats:
        c.wait()

    def side_sum(rnd, energy):
        side[rnd, 0] = energy
        copies = [
            remote(side.at[rnd, 0], side.at[rnd, k], side_send.at[rnd, k], side_recv.at[rnd, k], me ^ k, expert)
            for k in range(1, SIDE)
        ]
        for c in copies:
            c.start()
        for c in copies:
            c.wait()
        return jnp.sum(side[rnd], axis=0)

    def row_share(rnd, energy):
        rows[rnd, 0] = energy
        copies = [
            remote(rows.at[rnd, 0], rows.at[rnd, k], row_send.at[rnd, k], row_recv.at[rnd, k], me ^ (SIDE * k), expert)
            for k in range(1, NX)
        ]
        for c in copies:
            c.start()
        for c in copies:
            c.wait()

    groups, each, slot_count = feats.shape
    seqs = leaf_mix.shape[0]
    label = lax.broadcasted_iota(jnp.int32, (seqs, slot_count), 0).astype(F32)
    sums = []
    for g in range(groups):
        belongs = codes[g, 0:1] == label
        spread = jnp.concatenate(
            [jnp.where(belongs, feats[g, i : i + 1], 0.0).astype(BF16) for i in range(each)], axis=0
        )
        per_seq = jnp.dot(spread, grads[g], preferred_element_type=F32).astype(BF16)
        total = jnp.zeros((seqs, 128), F32)
        for h in range(each // 2):
            pair = jnp.concatenate([per_seq[(2 * h + b) * seqs : (2 * h + b + 1) * seqs] for b in range(2)], axis=1)
            mixed = jnp.dot(leaf_mix[...], pair, preferred_element_type=F32)
            nodes[g * 128 : (g + 1) * 128, h * 256 : (h + 1) * 256] = mixed.astype(BF16)
            total += mixed[:, :128] * mixed[:, :128] + mixed[:, 128:] * mixed[:, 128:]
        sums.append(jnp.sum(total, axis=1, keepdims=True))
    energy = side_sum(0, as_rows(sums, 8))

    source, target, count = nodes, nodes_b, groups
    for level in range(3):
        factor = factors(energy)
        sums = []
        for m in range(count // 2):
            weight = jnp.concatenate([factor[2 * m : 2 * m + 1], factor[2 * m + 1 : 2 * m + 2]], axis=1)
            weight = (merge_mix[...].astype(F32) * weight).astype(BF16)
            total = jnp.zeros((128, 128), F32)
            for h in range(NX):
                columns = slice(h * 256, (h + 1) * 256)
                mixed = jnp.dot(weight, source[m * 256 : (m + 1) * 256, columns], preferred_element_type=F32)
                target[m * 128 : (m + 1) * 128, columns] = mixed.astype(BF16)
                total += mixed[:, :128] * mixed[:, :128] + mixed[:, 128:] * mixed[:, 128:]
            sums.append(jnp.sum(total, axis=1, keepdims=True))
        source, target, count = target, source, count // 2
        if level == 2:
            for h in range(NX):
                lines[h] = source[0:128, h * 256 : (h + 1) * 256]
            shares = []
            for k in range(1, NX):
                shares.append(remote(
                    lines.at[x ^ k], corner.at[k], line_send.at[k], line_recv.at[k], me ^ (SIDE * k), expert
                ))
            for c in shares:
                c.start()
            corner[0] = lines[x]
        energy = side_sum(1 + level, as_rows(sums, 8))

    row_share(0, energy)
    for c in shares:
        c.wait()
    sums = []
    for m in range(2):
        low, high = x ^ (2 * m), x ^ (2 * m + 1)
        weight = [factors(rows[0, k][0:1]) for k in (low, high)]
        weight = (merge_mix[...].astype(F32) * jnp.concatenate(weight, axis=1)).astype(BF16)
        stacked = jnp.concatenate([corner[low], corner[high]], axis=0)
        mixed = jnp.dot(weight, stacked, preferred_element_type=F32)
        corner_b[m * 128 : (m + 1) * 128] = mixed.astype(BF16)
        sums.append(jnp.sum(mixed * mixed, axis=1, keepdims=True))
    row_share(1, side_sum(4, as_rows(sums, 8)))
    factor = factors(jnp.sum(rows[1], axis=0))
    weight = jnp.concatenate([factor[0:1], factor[1:2]], axis=1)
    weight = (merge_mix[...].astype(F32) * weight).astype(BF16)
    mixed = jnp.dot(weight, corner_b[...], preferred_element_type=F32)
    row_share(2, side_sum(5, as_rows([jnp.sum(mixed * mixed, axis=1, keepdims=True)], 8)))
    factor = factors(jnp.sum(rows[2], axis=0))
    factor = jnp.broadcast_to(factor[0:1], (128, 128)).T
    out[...] = (mixed * jnp.concatenate([factor, factor], axis=1)).astype(BF16)


def shards(tokens, routes, lengths, hidden_grad, proj_in, proj_out, leaf_mix, merge_mix):
    tok_dev, width = tokens.shape
    capacity, depth = hidden_grad.shape[3:]
    slot_count = NZ * capacity
    kin, kout = proj_in.shape[2], proj_out.shape[2]
    hbm = pl.BlockSpec(memory_space=pl.ANY)
    vmem = pl.BlockSpec(memory_space=pltpu.VMEM)
    dma = pltpu.SemaphoreType.DMA
    columns = kin * kout // SIDE
    result = pl.pallas_call(
        kernel,
        out_shape=jax.ShapeDtypeStruct((128, columns // NX), BF16),
        in_specs=[hbm, vmem, vmem, hbm, hbm, hbm, vmem, vmem],
        out_specs=vmem,
        scratch_shapes=[
            pltpu.VMEM((NC * tok_dev, width), BF16),
            pltpu.VMEM((kin, width // (NX * NY)), BF16),
            pltpu.VMEM((NX, NY, NZ * kin // NC, width // (NX * NY)), BF16),
            pltpu.VMEM((CHUNKS, slot_count, depth // CHUNKS), BF16),
            pltpu.VMEM((CHUNKS, depth // CHUNKS, kout), BF16),
            pltpu.VMEM((NC * tok_dev, NZ * kin // NC), F32),
            pltpu.VMEM((NC, NZ, tok_dev), F32),
            pltpu.VMEM((SIDE, 8, slot_count), F32),
            pltpu.VMEM((SIDE, slot_count, kout), BF16),
            pltpu.VMEM((NZ, NC, capacity, 128), BF16),
            pltpu.VMEM((NZ, NC, capacity, 128), BF16),
            pltpu.VMEM((NY, NC, 8, slot_count), F32),
            pltpu.VMEM((SIDE, 8, slot_count), F32),
            pltpu.VMEM((SIDE * 128, columns), BF16),
            pltpu.VMEM((SIDE * 64, columns), BF16),
            pltpu.VMEM((NX, 128, columns // NX), BF16),
            pltpu.VMEM((NX, 128, columns // NX), BF16),
            pltpu.VMEM((256, columns // NX), BF16),
            pltpu.VMEM((6, SIDE, 8, 128), F32),
            pltpu.VMEM((3, NX, 8, 128), F32),
            dma((2 + 2 * CHUNKS,)),
            dma((2,)),
            dma((2,)),
            dma((SIDE,)), dma((SIDE,)),
            dma((NY,)), dma((NY,)),
            dma((NY,)), dma((NY,)),
            dma((NZ,)), dma((NZ,)),
            dma((4, 4)), dma((4, 4)),
            dma((NZ,)), dma((NZ,)),
            dma((NY,)), dma((NY,)),
            dma((6, SIDE)), dma((6, SIDE)),
            dma((3, NX)), dma((3, NX)),
            dma((NX,)), dma((NX,)),
        ],
        compiler_params=pltpu.CompilerParams(
            collective_id=0, has_side_effects=True, vmem_limit_bytes=48 << 20
        ),
    )(
        tokens, routes.T, lengths[None], hidden_grad.reshape(slot_count, depth), proj_in[0].T, proj_out[0],
        leaf_mix, merge_mix,
    )
    return result[None]


def solution(mesh):
    in_specs = (
        P(("dp", "expert"), None),
        P("dp", None),
        P("dp"),
        P("dp", "expert", None, None, None),
        P("expert", None, None),
        P("expert", None, None),
        P(),
        P(),
    )
    out_specs = P("expert", None, "dp")
    return jax.shard_map(shards, mesh=mesh, in_specs=in_specs, out_specs=out_specs, check_vma=False)
```

```python
import jax
import jax.numpy as jnp
from jax import lax
from jax.experimental import pallas as pl
from jax.experimental.pallas import tpu as pltpu
from jax.sharding import PartitionSpec as P

SEQ_LEN = 8
EPSILON = 1e-06
MESH = pl.DeviceIdType.MESH
NX, NY, NC, NZ = 4, 4, 2, 8
SIDE = NY * NC
PLANE = NX * SIDE
CHUNKS = 8
F32 = jnp.float32
BF16 = jnp.bfloat16


def factors(energy):
    threshold = jnp.mean(energy, axis=-1, keepdims=True)
    return energy / (energy + threshold + EPSILON)


def remote(src, dst, send, recv, dp, expert):
    return pltpu.make_async_remote_copy(
        src_ref=src, dst_ref=dst, send_sem=send, recv_sem=recv,
        device_id={"dp": dp, "expert": expert}, device_id_type=MESH,
    )


def as_rows(column_sums, count):
    lane = lax.broadcasted_iota(jnp.int32, (128, 128), 1)
    square = jnp.zeros((128, 128), F32)
    for n, sums in enumerate(column_sums):
        square = jnp.where(lane == n, sums, square)
    return square.T[:count]


def kernel(
    tokens, routes_in, lengths_in, hidden, proj_in, proj_out, leaf_in, merge_in, out,
    routes, lengths, leaf_mix, merge_mix,
    both, raw, weights, grad_in, grad_mix, feature, places, codes, grads, sent, got, turned, feats,
    gram, products, mixes, chips, leaves, firsts,
    nodes, nodes_b, lines, corner, corner_b, side, plane, rows,
    local, token_sem, place_sem, code_send, code_recv, grad_send, grad_recv, pass_send, pass_recv,
    piece_send, piece_recv, ring_send, ring_recv, slot_send, slot_recv, feat_send, feat_recv,
    chip_sem, leaf_send, leaf_recv, first_send, first_recv,
    side_send, side_recv, plane_send, plane_recv, line_send, line_recv,
):
    me, expert = lax.axis_index("dp"), lax.axis_index("expert")
    x, y, core = me // SIDE, (me // NC) % NY, me % NC
    pair = me ^ 1
    n_expert = NZ
    tok_dev = tokens.shape[0]
    depth = tokens.shape[1] // (NX * NY)
    capacity = sent.shape[2]
    slot_count = n_expert * capacity
    half_kin = weights.shape[2] // n_expert

    spot = (x * NY + y) * depth
    load_piece = pltpu.make_async_copy(
        proj_in.at[:, pl.ds(pl.multiple_of(spot, 128), depth)], raw, local.at[0]
    )
    load_piece.start()
    small = [
        pltpu.make_async_copy(a, b, local.at[2 + 2 * CHUNKS + n])
        for n, (a, b) in enumerate(
            ((routes_in, routes), (lengths_in, lengths), (leaf_in, leaf_mix), (merge_in, merge_mix))
        )
    ]
    for c in small:
        c.start()
    own_rows = pl.ds(pl.multiple_of(core * tok_dev, tok_dev), tok_dev)
    load_tokens = pltpu.make_async_copy(tokens, both.at[own_rows], local.at[1])
    chunk = hidden.shape[1] // CHUNKS
    loads = []
    for n in range(CHUNKS):
        part = slice(n * chunk, (n + 1) * chunk)
        loads.append((
            pltpu.make_async_copy(hidden.at[:, part], grad_in.at[n], local.at[2 + 2 * n]),
            pltpu.make_async_copy(proj_out.at[part], grad_mix.at[n], local.at[3 + 2 * n]),
        ))
    for pair_of_loads in loads:
        for c in pair_of_loads:
            c.start()
    load_tokens.start()

    barrier = pltpu.get_barrier_semaphore()
    peers = [me ^ k for k in range(1, PLANE)]
    for peer in peers:
        pl.semaphore_signal(barrier, inc=1, device_id={"dp": peer, "expert": expert}, device_id_type=MESH)
    for k in range(1, NZ):
        pl.semaphore_signal(barrier, inc=1, device_id={"dp": me, "expert": expert ^ k}, device_id_type=MESH)
    pl.semaphore_wait(barrier, len(peers) + NZ - 1)

    load_piece.wait()
    r = lax.broadcasted_iota(jnp.int32, (half_kin, 2 * half_kin), 0)
    c = lax.broadcasted_iota(jnp.int32, (half_kin, 2 * half_kin), 1)
    wanted = (r % 8) // 2 * 16 + r // 8 * 4 + core * 2 + r % 2
    pick = (wanted == c).astype(BF16)
    own_piece = weights.at[x, y, pl.ds(pl.multiple_of(expert * half_kin, half_kin), half_kin)]
    own_piece[...] = jnp.dot(pick, raw[...], preferred_element_type=F32).astype(BF16)
    pieces = [
        remote(own_piece, own_piece, piece_send.at[k], piece_recv.at[k], me, expert ^ k)
        for k in range(1, NZ)
    ]
    for c in pieces:
        c.start()
    share_tokens = remote(tokens, both.at[own_rows], token_sem.at[0], token_sem.at[1], pair, expert)
    share_tokens.start()

    for c in small:
        c.wait()
    r = lax.broadcasted_iota(jnp.int32, (tok_dev, tok_dev), 0)
    c = lax.broadcasted_iota(jnp.int32, (tok_dev, tok_dev), 1)
    earlier = (r < c).astype(BF16)
    seq_dev = tok_dev // SEQ_LEN
    lasting = jnp.broadcast_to(lengths[...], (8, tok_dev)).astype(F32).astype(BF16)
    owner = (r == expert * seq_dev + c // SEQ_LEN).astype(BF16)
    lasting = jnp.dot(lasting, owner, preferred_element_type=F32)
    r = lax.broadcasted_iota(jnp.int32, (8, tok_dev), 0)
    c = lax.broadcasted_iota(jnp.int32, (8, tok_dev), 1)
    live = (c % SEQ_LEN).astype(F32) < lasting

    def placed(match):
        before = jnp.dot(match.astype(F32).astype(BF16), earlier, preferred_element_type=F32)
        return jnp.where(match, before, -1.0)

    here = pl.ds(pl.multiple_of(expert * tok_dev, tok_dev), tok_dev)
    match = (routes[0:1, here] == r) | (routes[1:2, here] == r)
    places[core] = jnp.where(live, placed(match), -1.0)
    share_places = remote(places.at[core], places.at[core], place_sem.at[0], place_sem.at[1], pair, expert)
    share_places.start()
    first = jnp.concatenate([routes[0:1, j * tok_dev : (j + 1) * tok_dev] for j in range(n_expert)], axis=0)
    second = jnp.concatenate([routes[1:2, j * tok_dev : (j + 1) * tok_dev] for j in range(n_expert)], axis=0)
    place = placed((first == expert) | (second == expert))
    cell = lax.broadcasted_iota(jnp.int32, (capacity, tok_dev), 0).astype(F32)
    held = jnp.concatenate([(place[j : j + 1] == cell).astype(F32).astype(BF16) for j in range(n_expert)], axis=0)
    number = (c // SEQ_LEN).astype(F32).astype(BF16)
    code = lax.dot_general(number, held, (((1,), (1,)), ((), ())), preferred_element_type=F32)
    source = lax.broadcasted_iota(jnp.int32, (8, slot_count), 1) // capacity
    group = me % SIDE
    codes[group] = code + (source * seq_dev).astype(F32)
    share_codes = [
        remote(codes.at[group], codes.at[group], code_send.at[k], code_recv.at[k], me ^ k, expert)
        for k in range(1, SIDE)
    ]
    for c in share_codes:
        c.start()

    total = jnp.zeros((slot_count, grads.shape[2]), F32)
    for n in range(CHUNKS):
        for c in loads[n]:
            c.wait()
        total += jnp.dot(grad_in[n], grad_mix[n], preferred_element_type=F32)
    grads[group] = total.astype(BF16)

    share_pair = remote(grads.at[group], grads.at[group], grad_send.at[0], grad_recv.at[0], pair, expert)
    share_pair.start()

    for c in pieces:
        c.wait()
    up_x, down_x = (x + 1) % NX, (x + NX - 1) % NX
    up_y, down_y = (y + 1) % NY, (y + NY - 1) % NY
    at_x = lambda to: to * SIDE + y * NC + core
    at_y = lambda to: x * SIDE + to * NC + core
    half = weights.shape[2] // 2
    low, high = slice(0, half), slice(half, 2 * half)
    quarter = half // 2

    def along(block, n, target, up, down, own):
        there = []
        for way, to in enumerate((up, down)):
            there.append(remote(
                block(own, 0, half), block(own, 0, half), ring_send.at[n, way], ring_recv.at[n, way], target(to), expert
            ))
        for c in there:
            c.start()

        def onward():
            further = []
            for way, (to, came) in enumerate(((up, down), (down, up))):
                there[way].wait_recv()
                view = block(came, way * quarter, quarter)
                c = remote(view, view, ring_send.at[n, 2 + way], ring_recv.at[n, 2 + way], target(to), expert)
                c.start()
                further.append(c)
            return there + further

        return there, onward

    def finish(copies):
        for c in copies[:2]:
            c.wait_send()
        for c in copies[2:]:
            c.wait()

    _, onward_a = along(lambda i, s, w: weights.at[i, y, pl.ds(s, w)], 0, at_x, up_x, down_x, x)
    _, onward_b = along(lambda i, s, w: weights.at[x, i, pl.ds(half + s, w)], 1, at_y, up_y, down_y, y)
    copies_a, copies_b = onward_a(), onward_b()
    finish(copies_a)
    finish(copies_b)
    _, onward_a = along(lambda i, s, w: weights.at[:, i, pl.ds(s, w)], 2, at_y, up_y, down_y, y)
    _, onward_b = along(lambda i, s, w: weights.at[i, :, pl.ds(half + s, w)], 3, at_x, up_x, down_x, x)
    load_tokens.wait()
    share_tokens.wait()
    share_places.wait()
    for c in share_codes:
        c.wait()
    share_pair.wait()
    chip = group - core
    for h in range(NC):
        label = lax.broadcasted_iota(jnp.int32, (128, slot_count), 0).astype(F32)
        belongs = (codes[chip + h, 0:1] == label).astype(F32).astype(BF16)
        mixes[h] = jnp.dot(leaf_mix[...], belongs, preferred_element_type=F32).astype(BF16)
        for b in range(NC):
            gram[h, b] = lax.dot_general(
                grads[chip + h], grads[chip + b], (((1,), (1,)), ((), ())), preferred_element_type=F32
            )
    copies_a, copies_b = onward_a(), onward_b()
    finish(copies_a)
    finish(copies_b)
    share_grads = [
        remote(grads.at[group], grads.at[group], grad_send.at[k], grad_recv.at[k], me ^ (NC * k), expert)
        for k in range(1, NY)
    ]
    for c in share_grads:
        c.start()

    feature[...] = jnp.zeros_like(feature)
    for n in range(NX * NY):
        feature[...] += lax.dot_general(
            both[:, n * depth : (n + 1) * depth], weights[n // NY, n % NY],
            (((1,), (1,)), ((), ())), preferred_element_type=F32,
        )
    for h in range(NC):
        chosen = jnp.concatenate(
            [(places[h, e : e + 1] == cell).astype(F32).astype(BF16) for e in range(n_expert)], axis=0
        )
        slots = jnp.dot(chosen, feature[h * tok_dev : (h + 1) * tok_dev].astype(BF16), preferred_element_type=F32)
        for e in range(n_expert):
            lanes = e * half_kin // 128 * 128
            sent[e, h] = slots[e * capacity : (e + 1) * capacity, lanes : lanes + 128].astype(BF16)
    share_slots = [
        remote(sent.at[expert ^ k], got.at[expert], slot_send.at[k], slot_recv.at[k], me, expert ^ k)
        for k in range(1, NZ)
    ]
    for c in share_slots:
        c.start()
    got[expert] = sent[expert]
    pass_grads = []
    for k in range(1, NY):
        share_grads[k - 1].wait()
        far = group ^ (NC * k)
        c = remote(grads.at[far], grads.at[far], pass_send.at[k], pass_recv.at[k], pair, expert)
        c.start()
        pass_grads.append(c)
    for c in share_slots:
        c.wait()
    r = lax.broadcasted_iota(jnp.int32, (half_kin, 128), 0)
    c = lax.broadcasted_iota(jnp.int32, (half_kin, 128), 1)
    pick = (c == expert * half_kin % 128 + r).astype(BF16)
    mine = []
    for h in range(NC):
        everything = jnp.concatenate([got[j, h] for j in range(n_expert)], axis=0)
        lines_of = lax.dot_general(pick, everything, (((1,), (1,)), ((), ())), preferred_element_type=F32)
        mine.append(lines_of.astype(BF16))
        for to in range(NY):
            turned[to, h] = lines_of[to * 8 : (to + 1) * 8]
    share_feats = [
        remote(
            turned.at[y ^ k], feats.at[pl.ds(NC * y, NC)], feat_send.at[k], feat_recv.at[k], me ^ (NC * k), expert
        )
        for k in range(1, NY)
    ]
    for c in share_feats:
        c.start()
    feats[pl.ds(NC * y, NC)] = turned[y]

    for h in range(NC):
        for b in range(NC):
            alike = lax.dot_general(mine[h], mine[b], (((0,), (0,)), ((), ())), preferred_element_type=F32)
            products[h, b] = (alike * gram[h, b]).astype(BF16)
    sums = []
    for h in range(NC):
        mixed = jnp.dot(mixes[h], products[h, h], preferred_element_type=F32)
        sums.append(jnp.sum(mixed * mixes[h].astype(F32), axis=1, keepdims=True))
    chips[0] = as_rows(sums, 8)
    share_chip = remote(chips.at[0], chips.at[1], chip_sem.at[0], chip_sem.at[1], pair, expert)
    share_chip.start()
    share_chip.wait()
    energy = chips[0] + chips[1]
    leaves[y] = energy
    share_leaves = [
        remote(leaves.at[y], leaves.at[y], leaf_send.at[k], leaf_recv.at[k], me ^ (NC * k), expert)
        for k in range(1, NY)
    ]
    for c in share_leaves:
        c.start()
    factor = factors(energy)
    weight = jnp.concatenate([factor[0:1], factor[1:2]], axis=1)
    weight = (merge_mix[...].astype(F32) * weight).astype(BF16)
    reach = [
        jnp.dot(weight[:, h * 128 : (h + 1) * 128], mixes[h], preferred_element_type=F32).astype(BF16)
        for h in range(NC)
    ]
    total = jnp.zeros((128, 1), F32)
    for b in range(NC):
        mixed = jnp.dot(reach[0], products[0, b], preferred_element_type=F32)
        mixed += jnp.dot(reach[1], products[1, b], preferred_element_type=F32)
        total += jnp.sum(mixed * reach[b].astype(F32), axis=1, keepdims=True)
    firsts[group] = as_rows([total], 8)
    share_firsts = [
        remote(firsts.at[group], firsts.at[group], first_send.at[k], first_recv.at[k], me ^ k, expert)
        for k in range(1, SIDE)
    ]
    for c in share_firsts:
        c.start()
    for c in pass_grads:
        c.wait()
    for c in share_feats:
        c.wait()

    def side_sum(rnd, energy):
        side[rnd, 0] = energy
        copies = [
            remote(side.at[rnd, 0], side.at[rnd, k], side_send.at[rnd, k], side_recv.at[rnd, k], me ^ k, expert)
            for k in range(1, SIDE)
        ]
        for c in copies:
            c.start()
        for c in copies:
            c.wait()
        return jnp.sum(side[rnd], axis=0)

    def plane_share(rnd, energy):
        plane[rnd, 0] = energy
        copies = [
            remote(plane.at[rnd, 0], plane.at[rnd, k], plane_send.at[rnd, k], plane_recv.at[rnd, k], me ^ k, expert)
            for k in range(PLANE - 1, 0, -1)
        ]
        for c in copies:
            c.start()
        for c in copies:
            c.wait()

    groups, each, slot_count = feats.shape
    seqs = leaf_mix.shape[0]
    label = lax.broadcasted_iota(jnp.int32, (seqs, slot_count), 0).astype(F32)
    for g in range(groups):
        belongs = codes[g, 0:1] == label
        spread = jnp.concatenate(
            [jnp.where(belongs, feats[g, i : i + 1], 0.0).astype(BF16) for i in range(each)], axis=0
        )
        per_seq = jnp.dot(spread, grads[g], preferred_element_type=F32).astype(BF16)
        for h in range(each // 2):
            pair = jnp.concatenate([per_seq[(2 * h + b) * seqs : (2 * h + b + 1) * seqs] for b in range(2)], axis=1)
            mixed = jnp.dot(leaf_mix[...], pair, preferred_element_type=F32)
            nodes[g * 128 : (g + 1) * 128, h * 256 : (h + 1) * 256] = mixed.astype(BF16)
    source, target, count = nodes, nodes_b, groups
    for c in share_leaves:
        c.wait()
    factor = factors(jnp.concatenate([leaves[n, 0:NC] for n in range(NY)], axis=0))
    for level in range(3):
        sums = []
        for m in range(count // 2):
            weight = jnp.concatenate([factor[2 * m : 2 * m + 1], factor[2 * m + 1 : 2 * m + 2]], axis=1)
            weight = (merge_mix[...].astype(F32) * weight).astype(BF16)
            total = jnp.zeros((128, 128), F32)
            for h in range(NX):
                columns = slice(h * 256, (h + 1) * 256)
                mixed = jnp.dot(weight, source[m * 256 : (m + 1) * 256, columns], preferred_element_type=F32)
                target[m * 128 : (m + 1) * 128, columns] = mixed.astype(BF16)
                total += mixed[:, :128] * mixed[:, :128] + mixed[:, 128:] * mixed[:, 128:]
            sums.append(jnp.sum(total, axis=1, keepdims=True))
        source, target, count = target, source, count // 2
        if level == 0:
            for c in share_firsts:
                c.wait()
            factor = factors(
                jnp.concatenate([firsts[NC * n, 0:1] + firsts[NC * n + 1, 0:1] for n in range(NY)], axis=0)
            )
        if level == 1:
            factor = factors(side_sum(0, as_rows(sums, 8)))

    for h in range(NX):
        lines[h] = source[0:128, h * 256 : (h + 1) * 256]
    shares = [
        remote(lines.at[x ^ k], corner.at[k], line_send.at[k], line_recv.at[k], me ^ (SIDE * k), expert)
        for k in range(1, NX)
    ]
    for c in shares:
        c.start()
    corner[0] = lines[x]
    energy = as_rows(sums, 8)
    plane_share(0, jnp.concatenate([energy[0:1], energy[0:1]], axis=1))
    for k in range(NX):
        rows[k] = factors(jnp.sum(plane[0, k * SIDE : (k + 1) * SIDE], axis=0)[:, :128])
    for c in shares:
        c.wait()
    sums = []
    for m in range(2):
        low, high = x ^ (2 * m), x ^ (2 * m + 1)
        weight = jnp.concatenate([rows[low], rows[high]], axis=1)
        weight = (merge_mix[...].astype(F32) * weight).astype(BF16)
        stacked = jnp.concatenate([corner[low], corner[high]], axis=0)
        mixed = jnp.dot(weight, stacked, preferred_element_type=F32)
        corner_b[m * 128 : (m + 1) * 128] = mixed.astype(BF16)
        sums.append(jnp.sum(mixed * mixed, axis=1, keepdims=True))
    energy = as_rows(sums, 8)
    plane_share(1, jnp.concatenate([energy[0:1], energy[1:2]], axis=1))
    energy = jnp.sum(plane[1], axis=0)
    weight = jnp.concatenate([factors(energy[:, :128]), factors(energy[:, 128:])], axis=1)
    weight = (merge_mix[...].astype(F32) * weight).astype(BF16)
    mixed = jnp.dot(weight, corner_b[...], preferred_element_type=F32)
    energy = as_rows([jnp.sum(mixed * mixed, axis=1, keepdims=True)], 8)
    plane_share(2, jnp.concatenate([energy[0:1], energy[0:1]], axis=1))
    factor = factors(jnp.sum(plane[2], axis=0)[:, :128])
    factor = jnp.broadcast_to(factor, (128, 128)).T
    out[...] = (mixed * jnp.concatenate([factor, factor], axis=1)).astype(BF16)


def shards(tokens, routes, lengths, hidden_grad, proj_in, proj_out, leaf_mix, merge_mix):
    tok_dev, width = tokens.shape
    capacity, depth = hidden_grad.shape[3:]
    slot_count = NZ * capacity
    kin, kout = proj_in.shape[2], proj_out.shape[2]
    hbm = pl.BlockSpec(memory_space=pltpu.HBM)
    vmem = pl.BlockSpec(memory_space=pltpu.VMEM)
    dma = pltpu.SemaphoreType.DMA
    columns = kin * kout // SIDE
    result = pl.pallas_call(
        kernel,
        out_shape=jax.ShapeDtypeStruct((128, columns // NX), BF16),
        in_specs=[hbm] * 8,
        out_specs=vmem,
        scratch_shapes=[
            pltpu.VMEM((2, NZ * tok_dev), jnp.int32),
            pltpu.VMEM((1, tok_dev), jnp.int32),
            pltpu.VMEM((128, 128), BF16),
            pltpu.VMEM((128, 256), BF16),
            pltpu.VMEM((NC * tok_dev, width), BF16),
            pltpu.VMEM((kin, width // (NX * NY)), BF16),
            pltpu.VMEM((NX, NY, NZ * kin // NC, width // (NX * NY)), BF16),
            pltpu.VMEM((CHUNKS, slot_count, depth // CHUNKS), BF16),
            pltpu.VMEM((CHUNKS, depth // CHUNKS, kout), BF16),
            pltpu.VMEM((NC * tok_dev, NZ * kin // NC), F32),
            pltpu.VMEM((NC, NZ, tok_dev), F32),
            pltpu.VMEM((SIDE, 8, slot_count), F32),
            pltpu.VMEM((SIDE, slot_count, kout), BF16),
            pltpu.VMEM((NZ, NC, capacity, 128), BF16),
            pltpu.VMEM((NZ, NC, capacity, 128), BF16),
            pltpu.VMEM((NY, NC, 8, slot_count), F32),
            pltpu.VMEM((SIDE, 8, slot_count), F32),
            pltpu.VMEM((NC, NC, slot_count, slot_count), F32),
            pltpu.VMEM((NC, NC, slot_count, slot_count), BF16),
            pltpu.VMEM((NC, 128, slot_count), BF16),
            pltpu.VMEM((2, 8, 128), F32),
            pltpu.VMEM((NY, 8, 128), F32),
            pltpu.VMEM((SIDE, 8, 128), F32),
            pltpu.VMEM((SIDE * 128, columns), BF16),
            pltpu.VMEM((SIDE * 64, columns), BF16),
            pltpu.VMEM((NX, 128, columns // NX), BF16),
            pltpu.VMEM((NX, 128, columns // NX), BF16),
            pltpu.VMEM((256, columns // NX), BF16),
            pltpu.VMEM((1, SIDE, 8, 128), F32),
            pltpu.VMEM((3, PLANE, 1, 256), F32),
            pltpu.VMEM((NX, 1, 128), F32),
            dma((6 + 2 * CHUNKS,)),
            dma((2,)),
            dma((2,)),
            dma((SIDE,)), dma((SIDE,)),
            dma((NY,)), dma((NY,)),
            dma((NY,)), dma((NY,)),
            dma((NZ,)), dma((NZ,)),
            dma((4, 4)), dma((4, 4)),
            dma((NZ,)), dma((NZ,)),
            dma((NY,)), dma((NY,)),
            dma((2,)), dma((NY,)), dma((NY,)), dma((SIDE,)), dma((SIDE,)),
            dma((1, SIDE)), dma((1, SIDE)),
            dma((3, PLANE)), dma((3, PLANE)),
            dma((NX,)), dma((NX,)),
        ],
        compiler_params=pltpu.CompilerParams(
            collective_id=0, has_side_effects=True, vmem_limit_bytes=48 << 20
        ),
    )(
        tokens, routes.T, lengths[None], hidden_grad.reshape(slot_count, depth), proj_in[0].T, proj_out[0],
        leaf_mix, merge_mix,
    )
    return result[None]


def solution(mesh):
    in_specs = (
        P(("dp", "expert"), None),
        P("dp", None),
        P("dp"),
        P("dp", "expert", None, None, None),
        P("expert", None, None),
        P("expert", None, None),
        P(),
        P(),
    )
    out_specs = P("expert", None, "dp")
    return jax.shard_map(shards, mesh=mesh, in_specs=in_specs, out_specs=out_specs, check_vma=False)
```

```python
import jax
import jax.numpy as jnp
from jax import lax
from jax.experimental import pallas as pl
from jax.experimental.pallas import tpu as pltpu
from jax.sharding import PartitionSpec as P

SEQ_LEN = 8
EPSILON = 1e-06
MESH = pl.DeviceIdType.MESH
NX, NY, NC, NZ = 4, 4, 2, 8
SIDE = NY * NC
PLANE = NX * SIDE
CHUNKS = 8
HOPS = 20
FAR = (2, 6, 4, 3, 5)
F32 = jnp.float32
BF16 = jnp.bfloat16


def factors(energy):
    threshold = jnp.mean(energy, axis=-1, keepdims=True)
    return energy / (energy + threshold + EPSILON)


def remote(src, dst, send, recv, dp, expert):
    return pltpu.make_async_remote_copy(
        src_ref=src, dst_ref=dst, send_sem=send, recv_sem=recv,
        device_id={"dp": dp, "expert": expert}, device_id_type=MESH,
    )


def as_rows(column_sums, count):
    lane = lax.broadcasted_iota(jnp.int32, (128, 128), 1)
    square = jnp.zeros((128, 128), F32)
    for n, sums in enumerate(column_sums):
        square = jnp.where(lane == n, sums, square)
    return square.T[:count]


def kernel(
    tokens, routes_in, lengths_in, hidden, proj_in, proj_out, leaf_in, merge_in, out,
    routes, lengths, leaf_mix, merge_mix,
    both, raw, direct, weights, grad_in, grad_mix, feature, places, codes, grads, sent, got, turned, feats,
    gram, products, mixes, chips, leaves, firsts,
    nodes, nodes_b, lines, corner, corner_b, side, plane, rows,
    local, token_sem, place_sem, code_send, code_recv, grad_send, grad_recv, pass_send, pass_recv,
    piece_send, piece_recv, direct_send, direct_recv, ring_send, ring_recv, slot_send, slot_recv, feat_send, feat_recv,
    chip_sem, leaf_send, leaf_recv, first_send, first_recv,
    side_send, side_recv, plane_send, plane_recv, line_send, line_recv,
):
    me, expert = lax.axis_index("dp"), lax.axis_index("expert")
    x, y, core = me // SIDE, (me // NC) % NY, me % NC
    pair = me ^ 1
    n_expert = NZ
    tok_dev = tokens.shape[0]
    depth = tokens.shape[1] // (NX * NY)
    capacity = sent.shape[2]
    slot_count = n_expert * capacity
    half_kin = direct.shape[1]

    load_proj = pltpu.make_async_copy(proj_in, raw, local.at[0])
    load_proj.start()
    small = [
        pltpu.make_async_copy(a, b, local.at[2 + 2 * CHUNKS + n])
        for n, (a, b) in enumerate(
            ((routes_in, routes), (lengths_in, lengths), (leaf_in, leaf_mix), (merge_in, merge_mix))
        )
    ]
    for c in small:
        c.start()
    own_rows = pl.ds(pl.multiple_of(core * tok_dev, tok_dev), tok_dev)
    load_tokens = pltpu.make_async_copy(tokens, both.at[own_rows], local.at[1])
    chunk = hidden.shape[1] // CHUNKS
    loads = []
    for n in range(CHUNKS):
        part = slice(n * chunk, (n + 1) * chunk)
        loads.append((
            pltpu.make_async_copy(hidden.at[:, part], grad_in.at[n], local.at[2 + 2 * n]),
            pltpu.make_async_copy(proj_out.at[part], grad_mix.at[n], local.at[3 + 2 * n]),
        ))
    for pair_of_loads in loads:
        for c in pair_of_loads:
            c.start()
    load_tokens.start()

    barrier = pltpu.get_barrier_semaphore()
    peers = [me ^ k for k in range(1, PLANE)]
    for peer in peers:
        pl.semaphore_signal(barrier, inc=1, device_id={"dp": peer, "expert": expert}, device_id_type=MESH)
    for k in range(1, NZ):
        pl.semaphore_signal(barrier, inc=1, device_id={"dp": me, "expert": expert ^ k}, device_id_type=MESH)

    load_proj.wait()
    r = lax.broadcasted_iota(jnp.int32, (half_kin, 2 * half_kin), 0)
    c = lax.broadcasted_iota(jnp.int32, (half_kin, 2 * half_kin), 1)
    wanted = (r % 8) // 2 * 16 + r // 8 * 4 + core * 2 + r % 2
    pick = (wanted == c).astype(BF16)
    for n in range(NX):
        part = slice(n * NY * depth, (n + 1) * NY * depth)
        direct[0, :, part] = jnp.dot(pick, raw[:, part], preferred_element_type=F32).astype(BF16)
    direct[3] = jnp.zeros_like(direct[3])
    pl.semaphore_wait(barrier, len(peers) + NZ - 1)

    spot = pl.ds(pl.multiple_of((x * NY + y) * depth, 128), depth)
    pieces = [
        remote(
            direct.at[0, :, spot], weights.at[x, y, n * half_kin : (n + 1) * half_kin],
            piece_send.at[n], piece_recv.at[n], me, (expert + NZ - away) % NZ,
        )
        for n, away in enumerate(FAR)
    ]
    for c in pieces:
        c.start()
    share_tokens = remote(tokens, both.at[own_rows], token_sem.at[0], token_sem.at[1], pair, expert)
    share_tokens.start()

    for c in small:
        c.wait()
    r = lax.broadcasted_iota(jnp.int32, (tok_dev, tok_dev), 0)
    c = lax.broadcasted_iota(jnp.int32, (tok_dev, tok_dev), 1)
    earlier = (r < c).astype(BF16)
    seq_dev = tok_dev // SEQ_LEN
    lasting = jnp.broadcast_to(lengths[...], (8, tok_dev)).astype(F32).astype(BF16)
    owner = (r == expert * seq_dev + c // SEQ_LEN).astype(BF16)
    lasting = jnp.dot(lasting, owner, preferred_element_type=F32)
    r = lax.broadcasted_iota(jnp.int32, (8, tok_dev), 0)
    c = lax.broadcasted_iota(jnp.int32, (8, tok_dev), 1)
    live = (c % SEQ_LEN).astype(F32) < lasting

    def placed(match):
        before = jnp.dot(match.astype(F32).astype(BF16), earlier, preferred_element_type=F32)
        return jnp.where(match, before, -1.0)

    here = pl.ds(pl.multiple_of(expert * tok_dev, tok_dev), tok_dev)
    match = (routes[0:1, here] == r) | (routes[1:2, here] == r)
    places[core] = jnp.where(live, placed(match), -1.0)
    share_places = remote(places.at[core], places.at[core], place_sem.at[0], place_sem.at[1], pair, expert)
    share_places.start()
    first = jnp.concatenate([routes[0:1, j * tok_dev : (j + 1) * tok_dev] for j in range(n_expert)], axis=0)
    second = jnp.concatenate([routes[1:2, j * tok_dev : (j + 1) * tok_dev] for j in range(n_expert)], axis=0)
    place = placed((first == expert) | (second == expert))
    cell = lax.broadcasted_iota(jnp.int32, (capacity, tok_dev), 0).astype(F32)
    held = jnp.concatenate([(place[j : j + 1] == cell).astype(F32).astype(BF16) for j in range(n_expert)], axis=0)
    number = (c // SEQ_LEN).astype(F32).astype(BF16)
    code = lax.dot_general(number, held, (((1,), (1,)), ((), ())), preferred_element_type=F32)
    source = lax.broadcasted_iota(jnp.int32, (8, slot_count), 1) // capacity
    group = me % SIDE
    codes[group] = code + (source * seq_dev).astype(F32)
    share_codes = [
        remote(codes.at[group], codes.at[group], code_send.at[k], code_recv.at[k], me ^ k, expert)
        for k in range(1, SIDE)
    ]
    for c in share_codes:
        c.start()

    for c in pieces:
        c.wait()

    half, split = weights.shape[2] // 2, weights.shape[2] * 3 // 10

    def hop(h, source, part, target, n):
        start, size = ((0, half), (0, split), (split, half - split))[part]
        at_x, at_y = source if h == 0 else source[::-1]
        to_x, to_y = target if h == 0 else target[::-1]
        view = weights.at[at_x, at_y, pl.ds(h * half + start, size)]
        n += h * HOPS
        hops[n] = remote(view, view, ring_send.at[n], ring_recv.at[n], to_x * SIDE + to_y * NC + core, expert)
        hops[n].start()

    hops = {}
    spots = [(x, y), (y, x)]
    turn = lambda v, by: (v + by) % 4

    def first(h):
        a, b = spots[h]
        hop(h, (a, b), 0, (turn(a, 1), b), 0)
        hop(h, (a, b), 0, (turn(a, 3), b), 1)

    def first_on(h):
        a, b = spots[h]
        hops[h * HOPS].wait_recv()
        hop(h, (turn(a, 3), b), 1, (turn(a, 1), b), 2)
        hops[h * HOPS + 1].wait_recv()
        hop(h, (turn(a, 1), b), 2, (turn(a, 3), b), 3)

    def second(h, by):
        a, b = spots[h]
        hop(h, (turn(a, by), b), 0, (a, turn(b, 1)), 4 + 4 * by)
        hop(h, (turn(a, by), b), 0, (a, turn(b, 3)), 5 + 4 * by)

    def second_on(h, by):
        a, b = spots[h]
        n = 4 + 4 * by
        hops[h * HOPS + n].wait_recv()
        hop(h, (turn(a, by), turn(b, 3)), 1, (a, turn(b, 1)), n + 2)
        hops[h * HOPS + n + 1].wait_recv()
        hop(h, (turn(a, by), turn(b, 1)), 2, (a, turn(b, 3)), n + 3)

    for h in range(2):
        first(h)
    for h in range(2):
        second(h, 0)
    next_to = [
        remote(
            direct.at[0], direct.at[slot], direct_send.at[slot], direct_recv.at[slot], me, (expert + by) % NZ
        )
        for slot, by in ((1, NZ - 1), (2, 1))
    ]
    for c in next_to:
        c.start()

    total = jnp.zeros((slot_count, grads.shape[2]), F32)
    for n in range(CHUNKS):
        for c in loads[n]:
            c.wait()
        total += jnp.dot(grad_in[n], grad_mix[n], preferred_element_type=F32)
    grads[group] = total.astype(BF16)
    share_pair = remote(grads.at[group], grads.at[group], grad_send.at[0], grad_recv.at[0], pair, expert)
    share_pair.start()

    for h in range(2):
        first_on(h)
    for by in (3, 1):
        for h in range(2):
            second(h, by)
    for h in range(2):
        second_on(h, 0)

    share_places.wait()
    for c in share_codes:
        c.wait()
    share_pair.wait()
    chip = group - core
    for h in range(NC):
        label = lax.broadcasted_iota(jnp.int32, (128, slot_count), 0).astype(F32)
        belongs = (codes[chip + h, 0:1] == label).astype(F32).astype(BF16)
        mixes[h] = jnp.dot(leaf_mix[...], belongs, preferred_element_type=F32).astype(BF16)
        for b in range(NC):
            gram[h, b] = lax.dot_general(
                grads[chip + h], grads[chip + b], (((1,), (1,)), ((), ())), preferred_element_type=F32
            )

    for h in range(2):
        for n in (2, 3):
            hops[h * HOPS + n].wait_recv()
        second(h, 2)
    for by in (3, 1):
        for h in range(2):
            second_on(h, by)
    load_tokens.wait()
    share_tokens.wait()
    for c in next_to:
        c.wait()
    feature[...] = jnp.zeros_like(feature)
    near = NC * tok_dev // 2
    for n in range(NX * NY):
        part = slice(n * depth, (n + 1) * depth)
        feature[:, :near] += lax.dot_general(
            both[:, part], direct[:, :, part].reshape(near, depth),
            (((1,), (1,)), ((), ())), preferred_element_type=F32,
        )
    for h in range(2):
        second_on(h, 2)
    for h in range(2):
        for by in range(4):
            for n in (2, 3):
                hops[h * HOPS + 4 + 4 * by + n].wait_recv()
    for c in hops.values():
        c.wait_send()
    share_grads = [
        remote(grads.at[group], grads.at[group], grad_send.at[k], grad_recv.at[k], me ^ (NC * k), expert)
        for k in range(1, NY)
    ]
    for c in share_grads:
        c.start()

    for n in range(NX * NY):
        feature[:, near : near + 2 * half] += lax.dot_general(
            both[:, n * depth : (n + 1) * depth], weights[n // NY, n % NY],
            (((1,), (1,)), ((), ())), preferred_element_type=F32,
        )
    order = (0, 1, NZ - 1) + FAR
    bases = [n * half_kin for n in range(3)] + [near + n * half_kin for n in range(len(FAR))]
    for h in range(NC):
        chosen = jnp.concatenate(
            [(places[h, pl.ds((expert + by) % NZ, 1)] == cell).astype(F32).astype(BF16) for by in order], axis=0
        )
        slots = jnp.dot(chosen, feature[h * tok_dev : (h + 1) * tok_dev].astype(BF16), preferred_element_type=F32)
        for n, base in enumerate(bases):
            lanes, shift = base // 128 * 128, base % 128
            tile = slots[n * capacity : (n + 1) * capacity, lanes : lanes + 128]
            if shift:
                tile = pltpu.roll(tile, 128 - shift, 1)
            sent[n, h] = tile.astype(BF16)
    share_slots = [
        remote(sent.at[n], got.at[expert], slot_send.at[n], slot_recv.at[n], me, (expert + by) % NZ)
        for n, by in enumerate(order) if n
    ]
    for c in share_slots:
        c.start()
    got[expert] = sent[0]
    pass_grads = []
    for k in range(1, NY):
        share_grads[k - 1].wait()
        far = group ^ (NC * k)
        c = remote(grads.at[far], grads.at[far], pass_send.at[k], pass_recv.at[k], pair, expert)
        c.start()
        pass_grads.append(c)
    for c in share_slots:
        c.wait()
    r = lax.broadcasted_iota(jnp.int32, (half_kin, 128), 0)
    c = lax.broadcasted_iota(jnp.int32, (half_kin, 128), 1)
    pick = (c == r).astype(BF16)
    mine = []
    for h in range(NC):
        everything = jnp.concatenate([got[j, h] for j in range(n_expert)], axis=0)
        lines_of = lax.dot_general(pick, everything, (((1,), (1,)), ((), ())), preferred_element_type=F32)
        mine.append(lines_of.astype(BF16))
        for to in range(NY):
            turned[to, h] = lines_of[to * 8 : (to + 1) * 8]
    share_feats = [
        remote(
            turned.at[y ^ k], feats.at[pl.ds(NC * y, NC)], feat_send.at[k], feat_recv.at[k], me ^ (NC * k), expert
        )
        for k in range(1, NY)
    ]
    for c in share_feats:
        c.start()
    feats[pl.ds(NC * y, NC)] = turned[y]

    for h in range(NC):
        for b in range(NC):
            alike = lax.dot_general(mine[h], mine[b], (((0,), (0,)), ((), ())), preferred_element_type=F32)
            products[h, b] = (alike * gram[h, b]).astype(BF16)
    sums = []
    for h in range(NC):
        mixed = jnp.dot(mixes[h], products[h, h], preferred_element_type=F32)
        sums.append(jnp.sum(mixed * mixes[h].astype(F32), axis=1, keepdims=True))
    chips[0] = as_rows(sums, 8)
    share_chip = remote(chips.at[0], chips.at[1], chip_sem.at[0], chip_sem.at[1], pair, expert)
    share_chip.start()
    share_chip.wait()
    energy = chips[0] + chips[1]
    leaves[y] = energy
    share_leaves = [
        remote(leaves.at[y], leaves.at[y], leaf_send.at[k], leaf_recv.at[k], me ^ (NC * k), expert)
        for k in range(1, NY)
    ]
    for c in share_leaves:
        c.start()
    factor = factors(energy)
    weight = jnp.concatenate([factor[0:1], factor[1:2]], axis=1)
    weight = (merge_mix[...].astype(F32) * weight).astype(BF16)
    reach = [
        jnp.dot(weight[:, h * 128 : (h + 1) * 128], mixes[h], preferred_element_type=F32).astype(BF16)
        for h in range(NC)
    ]
    total = jnp.zeros((128, 1), F32)
    for b in range(NC):
        mixed = jnp.dot(reach[0], products[0, b], preferred_element_type=F32)
        mixed += jnp.dot(reach[1], products[1, b], preferred_element_type=F32)
        total += jnp.sum(mixed * reach[b].astype(F32), axis=1, keepdims=True)
    firsts[group] = as_rows([total], 8)
    share_firsts = [
        remote(firsts.at[group], firsts.at[group], first_send.at[k], first_recv.at[k], me ^ k, expert)
        for k in range(1, SIDE)
    ]
    for c in share_firsts:
        c.start()
    for c in pass_grads:
        c.wait()
    for c in share_feats:
        c.wait()

    def side_sum(rnd, energy):
        side[rnd, 0] = energy
        copies = [
            remote(side.at[rnd, 0], side.at[rnd, k], side_send.at[rnd, k], side_recv.at[rnd, k], me ^ k, expert)
            for k in range(1, SIDE)
        ]
        for c in copies:
            c.start()
        for c in copies:
            c.wait()
        return jnp.sum(side[rnd], axis=0)

    def plane_share(rnd, energy):
        plane[rnd, 0] = energy
        copies = [
            remote(plane.at[rnd, 0], plane.at[rnd, k], plane_send.at[rnd, k], plane_recv.at[rnd, k], me ^ k, expert)
            for k in range(PLANE - 1, 0, -1)
        ]
        for c in copies:
            c.start()
        for c in copies:
            c.wait()

    groups, each, slot_count = feats.shape
    seqs = leaf_mix.shape[0]
    label = lax.broadcasted_iota(jnp.int32, (seqs, slot_count), 0).astype(F32)
    for g in range(groups):
        belongs = codes[g, 0:1] == label
        spread = jnp.concatenate(
            [jnp.where(belongs, feats[g, i : i + 1], 0.0).astype(BF16) for i in range(each)], axis=0
        )
        per_seq = jnp.dot(spread, grads[g], preferred_element_type=F32).astype(BF16)
        for h in range(each // 2):
            pair = jnp.concatenate([per_seq[(2 * h + b) * seqs : (2 * h + b + 1) * seqs] for b in range(2)], axis=1)
            mixed = jnp.dot(leaf_mix[...], pair, preferred_element_type=F32)
            nodes[g * 128 : (g + 1) * 128, h * 256 : (h + 1) * 256] = mixed.astype(BF16)
    source, target, count = nodes, nodes_b, groups
    for c in share_leaves:
        c.wait()
    factor = factors(jnp.concatenate([leaves[n, 0:NC] for n in range(NY)], axis=0))
    for level in range(3):
        sums = []
        for m in range(count // 2):
            weight = jnp.concatenate([factor[2 * m : 2 * m + 1], factor[2 * m + 1 : 2 * m + 2]], axis=1)
            weight = (merge_mix[...].astype(F32) * weight).astype(BF16)
            total = jnp.zeros((128, 128), F32)
            for h in range(NX):
                columns = slice(h * 256, (h + 1) * 256)
                mixed = jnp.dot(weight, source[m * 256 : (m + 1) * 256, columns], preferred_element_type=F32)
                target[m * 128 : (m + 1) * 128, columns] = mixed.astype(BF16)
                total += mixed[:, :128] * mixed[:, :128] + mixed[:, 128:] * mixed[:, 128:]
            sums.append(jnp.sum(total, axis=1, keepdims=True))
        source, target, count = target, source, count // 2
        if level == 0:
            for c in share_firsts:
                c.wait()
            factor = factors(
                jnp.concatenate([firsts[NC * n, 0:1] + firsts[NC * n + 1, 0:1] for n in range(NY)], axis=0)
            )
        if level == 1:
            factor = factors(side_sum(0, as_rows(sums, 8)))

    for h in range(NX):
        lines[h] = source[0:128, h * 256 : (h + 1) * 256]
    shares = [
        remote(lines.at[x ^ k], corner.at[k], line_send.at[k], line_recv.at[k], me ^ (SIDE * k), expert)
        for k in range(1, NX)
    ]
    for c in shares:
        c.start()
    corner[0] = lines[x]
    energy = as_rows(sums, 8)
    plane_share(0, jnp.concatenate([energy[0:1], energy[0:1]], axis=1))
    for k in range(NX):
        rows[k] = factors(jnp.sum(plane[0, k * SIDE : (k + 1) * SIDE], axis=0)[:, :128])
    for c in shares:
        c.wait()
    sums = []
    for m in range(2):
        low, high = x ^ (2 * m), x ^ (2 * m + 1)
        weight = jnp.concatenate([rows[low], rows[high]], axis=1)
        weight = (merge_mix[...].astype(F32) * weight).astype(BF16)
        stacked = jnp.concatenate([corner[low], corner[high]], axis=0)
        mixed = jnp.dot(weight, stacked, preferred_element_type=F32)
        corner_b[m * 128 : (m + 1) * 128] = mixed.astype(BF16)
        sums.append(jnp.sum(mixed * mixed, axis=1, keepdims=True))
    energy = as_rows(sums, 8)
    plane_share(1, jnp.concatenate([energy[0:1], energy[1:2]], axis=1))
    energy = jnp.sum(plane[1], axis=0)
    weight = jnp.concatenate([factors(energy[:, :128]), factors(energy[:, 128:])], axis=1)
    weight = (merge_mix[...].astype(F32) * weight).astype(BF16)
    mixed = jnp.dot(weight, corner_b[...], preferred_element_type=F32)
    energy = as_rows([jnp.sum(mixed * mixed, axis=1, keepdims=True)], 8)
    plane_share(2, jnp.concatenate([energy[0:1], energy[0:1]], axis=1))
    factor = factors(jnp.sum(plane[2], axis=0)[:, :128])
    factor = jnp.broadcast_to(factor, (128, 128)).T
    out[...] = (mixed * jnp.concatenate([factor, factor], axis=1)).astype(BF16)


def shards(tokens, routes, lengths, hidden_grad, proj_in, proj_out, leaf_mix, merge_mix):
    tok_dev, width = tokens.shape
    capacity, depth = hidden_grad.shape[3:]
    slot_count = NZ * capacity
    kin, kout = proj_in.shape[2], proj_out.shape[2]
    hbm = pl.BlockSpec(memory_space=pltpu.HBM)
    vmem = pl.BlockSpec(memory_space=pltpu.VMEM)
    dma = pltpu.SemaphoreType.DMA
    columns = kin * kout // SIDE
    result = pl.pallas_call(
        kernel,
        out_shape=jax.ShapeDtypeStruct((128, columns // NX), BF16),
        in_specs=[hbm] * 8,
        out_specs=vmem,
        scratch_shapes=[
            pltpu.VMEM((2, NZ * tok_dev), jnp.int32),
            pltpu.VMEM((1, tok_dev), jnp.int32),
            pltpu.VMEM((128, 128), BF16),
            pltpu.VMEM((128, 256), BF16),
            pltpu.VMEM((NC * tok_dev, width), BF16),
            pltpu.VMEM((kin, width), BF16),
            pltpu.VMEM((4, kin // NC, width), BF16),
            pltpu.VMEM((NX, NY, len(FAR) * kin // NC, width // (NX * NY)), BF16),
            pltpu.VMEM((CHUNKS, slot_count, depth // CHUNKS), BF16),
            pltpu.VMEM((CHUNKS, depth // CHUNKS, kout), BF16),
            pltpu.VMEM((NC * tok_dev, 384), F32),
            pltpu.VMEM((NC, NZ, tok_dev), F32),
            pltpu.VMEM((SIDE, 8, slot_count), F32),
            pltpu.VMEM((SIDE, slot_count, kout), BF16),
            pltpu.VMEM((NZ, NC, capacity, 128), BF16),
            pltpu.VMEM((NZ, NC, capacity, 128), BF16),
            pltpu.VMEM((NY, NC, 8, slot_count), F32),
            pltpu.VMEM((SIDE, 8, slot_count), F32),
            pltpu.VMEM((NC, NC, slot_count, slot_count), F32),
            pltpu.VMEM((NC, NC, slot_count, slot_count), BF16),
            pltpu.VMEM((NC, 128, slot_count), BF16),
            pltpu.VMEM((2, 8, 128), F32),
            pltpu.VMEM((NY, 8, 128), F32),
            pltpu.VMEM((SIDE, 8, 128), F32),
            pltpu.VMEM((SIDE * 128, columns), BF16),
            pltpu.VMEM((SIDE * 64, columns), BF16),
            pltpu.VMEM((NX, 128, columns // NX), BF16),
            pltpu.VMEM((NX, 128, columns // NX), BF16),
            pltpu.VMEM((256, columns // NX), BF16),
            pltpu.VMEM((1, SIDE, 8, 128), F32),
            pltpu.VMEM((3, PLANE, 1, 256), F32),
            pltpu.VMEM((NX, 1, 128), F32),
            dma((6 + 2 * CHUNKS,)),
            dma((2,)),
            dma((2,)),
            dma((SIDE,)), dma((SIDE,)),
            dma((NY,)), dma((NY,)),
            dma((NY,)), dma((NY,)),
            dma((NZ,)), dma((NZ,)),
            dma((3,)), dma((3,)),
            dma((2 * HOPS,)), dma((2 * HOPS,)),
            dma((NZ,)), dma((NZ,)),
            dma((NY,)), dma((NY,)),
            dma((2,)), dma((NY,)), dma((NY,)), dma((SIDE,)), dma((SIDE,)),
            dma((1, SIDE)), dma((1, SIDE)),
            dma((3, PLANE)), dma((3, PLANE)),
            dma((NX,)), dma((NX,)),
        ],
        compiler_params=pltpu.CompilerParams(
            collective_id=0, has_side_effects=True, vmem_limit_bytes=58 << 20
        ),
    )(
        tokens, routes.T, lengths[None], hidden_grad.reshape(slot_count, depth), proj_in[0].T, proj_out[0],
        leaf_mix, merge_mix,
    )
    return result[None]


def solution(mesh):
    in_specs = (
        P(("dp", "expert"), None),
        P("dp", None),
        P("dp"),
        P("dp", "expert", None, None, None),
        P("expert", None, None),
        P("expert", None, None),
        P(),
        P(),
    )
    out_specs = P("expert", None, "dp")
    return jax.shard_map(shards, mesh=mesh, in_specs=in_specs, out_specs=out_specs, check_vma=False)
```

```python
import jax
import jax.numpy as jnp
from jax import lax
from jax.experimental import pallas as pl
from jax.experimental.pallas import tpu as pltpu
from jax.sharding import PartitionSpec as P

SEQ_LEN = 8
EPSILON = 1e-06
MESH = pl.DeviceIdType.MESH
NX, NY, NC, NZ = 4, 4, 2, 8
SIDE = NY * NC
PLANE = NX * SIDE
CHUNKS = 8
HOPS = 20
DISTANCE = (0, 1, 2, 1)
OUTWARD = sorted(range(1, PLANE), key=lambda k: (-DISTANCE[k // SIDE] - DISTANCE[k // NC % NY], -k))
FAR = (2, 6, 3, 5, 4)
PIECES = ((0, 1), (2, 3, 4))
BATCHES = ((0, 32, 16), (64, 48, 32))
F32 = jnp.float32
BF16 = jnp.bfloat16


def factors(energy):
    threshold = jnp.mean(energy, axis=-1, keepdims=True)
    return energy / (energy + threshold + EPSILON)


def remote(src, dst, send, recv, dp, expert):
    return pltpu.make_async_remote_copy(
        src_ref=src, dst_ref=dst, send_sem=send, recv_sem=recv,
        device_id={"dp": dp, "expert": expert}, device_id_type=MESH,
    )


def as_rows(column_sums, count):
    lane = lax.broadcasted_iota(jnp.int32, (128, 128), 1)
    square = jnp.zeros((128, 128), F32)
    for n, sums in enumerate(column_sums):
        square = jnp.where(lane == n, sums, square)
    return square.T[:count]


def kernel(
    tokens, routes_in, lengths_in, hidden, proj_in, proj_out, leaf_in, merge_in, out,
    routes, lengths, leaf_mix, merge_mix,
    both, raw, direct, weights, grad_in, grad_mix, feature, places, codes, grads, sent, got, total, turned, feats,
    gram, products, mixes, leaves,
    nodes, nodes_b, lines, corner, corner_b, side, plane, rows,
    local, token_sem, place_sem, code_send, code_recv, grad_send, grad_recv, pass_send, pass_recv,
    piece_send, piece_recv, direct_send, direct_recv, ring_send, ring_recv, slot_send, slot_recv, feat_send, feat_recv,
    leaf_send, leaf_recv,
    side_send, side_recv, plane_send, plane_recv, line_send, line_recv,
):
    me, expert = lax.axis_index("dp"), lax.axis_index("expert")
    x, y, core = me // SIDE, (me // NC) % NY, me % NC
    pair = me ^ 1
    n_expert = NZ
    tok_dev = tokens.shape[0]
    depth = tokens.shape[1] // (NX * NY)
    capacity = total.shape[0] // NZ
    slot_count = n_expert * capacity
    half_kin = direct.shape[1]

    barrier = pltpu.get_barrier_semaphore()
    peers = [me ^ k for k in range(1, PLANE)]
    for peer in peers:
        pl.semaphore_signal(barrier, inc=1, device_id={"dp": peer, "expert": expert}, device_id_type=MESH)
    for k in range(1, NZ):
        for to in (me, pair):
            pl.semaphore_signal(barrier, inc=1, device_id={"dp": to, "expert": expert ^ k}, device_id_type=MESH)

    load_proj = pltpu.make_async_copy(proj_in, raw, local.at[0])
    load_proj.start()
    small = [
        pltpu.make_async_copy(a, b, local.at[2 + 2 * CHUNKS + n])
        for n, (a, b) in enumerate(
            ((routes_in, routes), (lengths_in, lengths), (leaf_in, leaf_mix), (merge_in, merge_mix))
        )
    ]
    for c in small:
        c.start()
    own_rows = pl.ds(pl.multiple_of(core * tok_dev, tok_dev), tok_dev)
    load_tokens = pltpu.make_async_copy(tokens, both.at[own_rows], local.at[1])
    chunk = hidden.shape[1] // CHUNKS
    loads = []
    for n in range(CHUNKS):
        part = slice(n * chunk, (n + 1) * chunk)
        loads.append((
            pltpu.make_async_copy(hidden.at[:, part], grad_in.at[n], local.at[2 + 2 * n]),
            pltpu.make_async_copy(proj_out.at[part], grad_mix.at[n], local.at[3 + 2 * n]),
        ))
    for pair_of_loads in loads:
        for c in pair_of_loads:
            c.start()
    load_tokens.start()

    load_proj.wait()
    r = lax.broadcasted_iota(jnp.int32, (half_kin, 2 * half_kin), 0)
    c = lax.broadcasted_iota(jnp.int32, (half_kin, 2 * half_kin), 1)
    wanted = (r % 8) // 2 * 16 + r // 8 * 4 + core * 2 + r % 2
    pick = (wanted == c).astype(BF16)
    for n in range(NX):
        part = slice(n * NY * depth, (n + 1) * NY * depth)
        direct[0, :, part] = jnp.dot(pick, raw[:, part], preferred_element_type=F32).astype(BF16)
    direct[3] = jnp.zeros_like(direct[3])
    pl.semaphore_wait(barrier, len(peers) + NC * (NZ - 1))

    spot = pl.ds(pl.multiple_of((x * NY + y) * depth, 128), depth)
    pieces = [
        remote(
            direct.at[0, :, spot], weights.at[x, y, n * half_kin : (n + 1) * half_kin],
            piece_send.at[n], piece_recv.at[n], me, (expert + NZ - away) % NZ,
        )
        for n, away in enumerate(FAR)
    ]
    for n in (4, 2, 3, 0, 1):
        pieces[n].start()
    share_tokens = remote(tokens, both.at[own_rows], token_sem.at[0], token_sem.at[1], pair, expert)
    share_tokens.start()

    for c in small:
        c.wait()
    r = lax.broadcasted_iota(jnp.int32, (tok_dev, tok_dev), 0)
    c = lax.broadcasted_iota(jnp.int32, (tok_dev, tok_dev), 1)
    earlier = (r < c).astype(BF16)
    seq_dev = tok_dev // SEQ_LEN
    lasting = jnp.broadcast_to(lengths[...], (8, tok_dev)).astype(F32).astype(BF16)
    owner = (r == expert * seq_dev + c // SEQ_LEN).astype(BF16)
    lasting = jnp.dot(lasting, owner, preferred_element_type=F32)
    r = lax.broadcasted_iota(jnp.int32, (8, tok_dev), 0)
    c = lax.broadcasted_iota(jnp.int32, (8, tok_dev), 1)
    live = (c % SEQ_LEN).astype(F32) < lasting

    def placed(match):
        before = jnp.dot(match.astype(F32).astype(BF16), earlier, preferred_element_type=F32)
        return jnp.where(match, before, -1.0)

    here = pl.ds(pl.multiple_of(expert * tok_dev, tok_dev), tok_dev)
    match = (routes[0:1, here] == r) | (routes[1:2, here] == r)
    places[core] = jnp.where(live, placed(match), -1.0)
    share_places = remote(places.at[core], places.at[core], place_sem.at[0], place_sem.at[1], pair, expert)
    share_places.start()
    first = jnp.concatenate([routes[0:1, j * tok_dev : (j + 1) * tok_dev] for j in range(n_expert)], axis=0)
    second = jnp.concatenate([routes[1:2, j * tok_dev : (j + 1) * tok_dev] for j in range(n_expert)], axis=0)
    place = placed((first == expert) | (second == expert))
    cell = lax.broadcasted_iota(jnp.int32, (capacity, tok_dev), 0).astype(F32)
    few = capacity // 2
    halves = [slice(s * few, (s + 1) * few) for s in range(2)]
    held = jnp.concatenate(
        [(place[j : j + 1] == cell[rows_of]).astype(F32) for rows_of in halves for j in range(n_expert)], axis=0
    ).astype(BF16)
    number = (c // SEQ_LEN).astype(F32).astype(BF16)
    code = lax.dot_general(number, held, (((1,), (1,)), ((), ())), preferred_element_type=F32)
    source = lax.broadcasted_iota(jnp.int32, (8, slot_count), 1) // few % n_expert
    group = me % SIDE
    codes[group] = code + (source * seq_dev).astype(F32)
    share_codes = [
        remote(codes.at[group], codes.at[group], code_send.at[k], code_recv.at[k], me ^ k, expert)
        for k in range(1, SIDE)
    ]
    for c in share_codes:
        c.start()

    def hop(t, h, source, part, target, n):
        _, half, split = BATCHES[t]
        start, size = ((0, half), (0, split), (split, half - split))[part]
        start += BATCHES[t][0] + h * half
        at_x, at_y = source if h == 0 else source[::-1]
        to_x, to_y = target if h == 0 else target[::-1]
        view = weights.at[at_x, at_y, pl.ds(start, size)]
        n += (2 * t + h) * HOPS
        hops[n] = remote(view, view, ring_send.at[n], ring_recv.at[n], to_x * SIDE + to_y * NC + core, expert)
        hops[n].start()

    hops = {}
    spots = [(x, y), (y, x)]
    turn = lambda v, by: (v + by) % 4

    def first(t, h):
        a, b = spots[h]
        for n, by in enumerate((2, 1, 3)):
            hop(t, h, (a, b), 0, (turn(a, by), b), n)

    def first_on(t, h):
        hops[(2 * t + h) * HOPS + 1].wait_recv()
        hops[(2 * t + h) * HOPS + 2].wait_recv()

    def second(t, h, by):
        a, b = spots[h]
        hop(t, h, (turn(a, by), b), 0, (a, turn(b, 1)), 4 + 4 * by)
        hop(t, h, (turn(a, by), b), 0, (a, turn(b, 3)), 5 + 4 * by)

    def second_on(t, h, by):
        a, b = spots[h]
        n = 4 + 4 * by
        hops[(2 * t + h) * HOPS + n].wait_recv()
        hop(t, h, (turn(a, by), turn(b, 3)), 1, (a, turn(b, 1)), n + 2)
        hops[(2 * t + h) * HOPS + n + 1].wait_recv()
        hop(t, h, (turn(a, by), turn(b, 1)), 2, (a, turn(b, 3)), n + 3)

    def begin(t):
        if t >= len(BATCHES):
            return
        for n in PIECES[t]:
            pieces[n].wait()
        for h in range(2):
            first(t, h)
        for h in range(2):
            second(t, h, 0)

    def go_on(t, step):
        if t >= len(BATCHES):
            return
        for h in range(2):
            if step == 0:
                first_on(t, h)
                second(t, h, 3)
                second(t, h, 1)
            if step == 1:
                hops[(2 * t + h) * HOPS].wait_recv()
                second(t, h, 2)
        for by in ((0,), (3, 1), (2,))[step]:
            for h in range(2):
                second_on(t, h, by)

    def gradients(n):
        for c in loads[n]:
            c.wait()
        product = jnp.dot(grad_in[n], grad_mix[n], preferred_element_type=F32)
        total[...] = product + total[...] if n else product

    begin(0)
    begin(1)
    next_to = [
        remote(
            direct.at[0], direct.at[slot], direct_send.at[slot], direct_recv.at[slot], me, (expert + by) % NZ
        )
        for slot, by in ((1, NZ - 1), (2, 1))
    ]
    for c in next_to:
        c.start()
    gradients(0)
    gradients(1)
    go_on(0, 0)
    begin(2)
    gradients(2)
    gradients(3)
    go_on(1, 0)
    gradients(4)
    go_on(0, 1)
    gradients(5)
    gradients(6)
    go_on(2, 0)
    gradients(7)
    grads[group] = jnp.concatenate(
        [total[j * capacity + s * few : j * capacity + (s + 1) * few] for s in range(2) for j in range(n_expert)], axis=0
    ).astype(BF16)
    share_pair = remote(grads.at[group], grads.at[group], grad_send.at[0], grad_recv.at[0], pair, expert)
    share_pair.start()
    go_on(1, 1)
    go_on(0, 2)
    share_places.wait()
    for c in share_codes:
        c.wait()
    share_pair.wait()
    chip = group - core
    for h in range(NC):
        label = lax.broadcasted_iota(jnp.int32, (128, slot_count), 0).astype(F32)
        belongs = (codes[chip + h, 0:1] == label).astype(F32).astype(BF16)
        mixes[h] = jnp.dot(leaf_mix[...], belongs, preferred_element_type=F32).astype(BF16)
    go_on(2, 1)
    for h in range(NC):
        for b in range(NC):
            gram[h, b] = lax.dot_general(
                grads[chip + h], grads[chip + b], (((1,), (1,)), ((), ())), preferred_element_type=F32
            )
    go_on(1, 2)
    go_on(2, 2)
    load_tokens.wait()
    share_tokens.wait()
    for c in next_to:
        c.wait()
    feature[...] = jnp.zeros_like(feature)
    near = NC * tok_dev // 2
    for n in range(NX * NY):
        part = slice(n * depth, (n + 1) * depth)
        feature[:, :near] += lax.dot_general(
            both[:, part], direct[:, :, part].reshape(near, depth),
            (((1,), (1,)), ((), ())), preferred_element_type=F32,
        )
    def far(by_x, by_y):
        at_x, at_y = turn(x, by_x), turn(y, by_y)
        part = pl.ds(pl.multiple_of((at_x * NY + at_y) * depth, 128), depth)
        feature[:, near : near + weights.shape[2]] += lax.dot_general(
            both[:, part], weights[at_x, at_y], (((1,), (1,)), ((), ())), preferred_element_type=F32
        )

    for by_x in (0, 1, 3):
        for by_y in (0, 1, 3):
            far(by_x, by_y)
    for t in range(len(BATCHES)):
        for h in range(2):
            for by in range(4):
                for n in (2, 3):
                    hops[(2 * t + h) * HOPS + 4 + 4 * by + n].wait_recv()
    for c in hops.values():
        c.wait_send()
    share_grads = [
        remote(grads.at[group], grads.at[group], grad_send.at[k], grad_recv.at[k], me ^ (NC * k), expert)
        for k in range(1, NY)
    ]
    for c in share_grads:
        c.start()

    for by in (0, 1, 3):
        far(2, by)
        far(by, 2)
    far(2, 2)
    order = (0, 1, NZ - 1) + FAR
    bases = [n * half_kin for n in range(3)] + [near + n * half_kin for n in range(len(FAR))]
    block = lax.broadcasted_iota(jnp.int32, (few, 128), 1) // half_kin
    slots = []
    for h in range(NC):
        chosen = jnp.concatenate(
            [(places[h, pl.ds((expert + by) % NZ, 1)] == cell).astype(F32).astype(BF16) for by in order], axis=0
        )
        slots.append(
            jnp.dot(chosen, feature[h * tok_dev : (h + 1) * tok_dev].astype(BF16), preferred_element_type=F32)
        )
    for n, base in enumerate(bases):
        lanes = base // 128 * 128
        tile = jnp.zeros((few, 128), F32)
        for h in range(NC):
            for s in range(2):
                at = n * capacity + s * few
                there = 2 * h + s
                piece = slots[h][at : at + few, lanes : lanes + 128]
                shift = (there * half_kin - base) % 128
                tile = jnp.where(block == there, pltpu.roll(piece, shift, 1) if shift else piece, tile)
        sent[n] = jnp.concatenate([tile, jnp.zeros((sent.shape[1] - few, 128), F32)], axis=0).astype(BF16)
    share_slots = [
        remote(
            sent.at[n], got.at[core, expert], slot_send.at[to, n], slot_recv.at[to, n], pair if to else me,
            (expert + by) % NZ,
        )
        for n, by in reversed(list(enumerate(order))) for to in range(NC) if n or to
    ]
    for c in share_slots:
        c.start()
    got[core, expert] = sent[0]
    pass_grads = []
    for k in range(1, NY):
        share_grads[k - 1].wait()
        far = group ^ (NC * k)
        c = remote(grads.at[far], grads.at[far], pass_send.at[k], pass_recv.at[k], pair, expert)
        c.start()
        pass_grads.append(c)
    for c in share_slots:
        c.wait()
    r = lax.broadcasted_iota(jnp.int32, (half_kin, 128), 0)
    c = lax.broadcasted_iota(jnp.int32, (half_kin, 128), 1)
    pick = (c == r).astype(BF16)
    mine = [[], []]
    for to in range(NC):
        whose = core ^ to
        packed = jnp.concatenate([got[whose, j].astype(F32)[:few] for j in range(n_expert)], axis=0)
        for h in range(NC):
            everything = jnp.concatenate(
                [packed if h + s == 0 else pltpu.roll(packed, 128 - (2 * h + s) * half_kin, 1) for s in range(2)],
                axis=0,
            ).astype(BF16)
            lines_of = lax.dot_general(pick, everything, (((1,), (1,)), ((), ())), preferred_element_type=F32)
            mine[h].append(lines_of.astype(BF16))
            if to == 0:
                for there in range(NY):
                    turned[there, h] = lines_of[there * 8 : (there + 1) * 8]
        if to == 0:
            share_feats = [
                remote(
                    turned.at[y ^ k], feats.at[pl.ds(NC * y, NC)], feat_send.at[k], feat_recv.at[k], me ^ (NC * k), expert
                )
                for k in range(1, NY)
            ]
            for c in share_feats:
                c.start()
    feats[pl.ds(NC * y, NC)] = turned[y]

    full = [jnp.concatenate(mine[h], axis=0) for h in range(NC)]
    for h in range(NC):
        for b in range(NC):
            alike = lax.dot_general(full[h], full[b], (((0,), (0,)), ((), ())), preferred_element_type=F32)
            products[h, b] = (alike * gram[h, b]).astype(BF16)
    sums = []
    for h in range(NC):
        mixed = jnp.dot(mixes[h], products[h, h], preferred_element_type=F32)
        sums.append(jnp.sum(mixed * mixes[h].astype(F32), axis=1, keepdims=True))
    energy = as_rows(sums, 8)
    factor = factors(energy)
    weight = jnp.concatenate([factor[0:1], factor[1:2]], axis=1)
    weight = (merge_mix[...].astype(F32) * weight).astype(BF16)
    reach = [
        jnp.dot(weight[:, h * 128 : (h + 1) * 128], mixes[h], preferred_element_type=F32).astype(BF16)
        for h in range(NC)
    ]
    second_energy = jnp.zeros((128, 1), F32)
    for b in range(NC):
        mixed = jnp.dot(reach[0], products[0, b], preferred_element_type=F32)
        mixed += jnp.dot(reach[1], products[1, b], preferred_element_type=F32)
        second_energy += jnp.sum(mixed * reach[b].astype(F32), axis=1, keepdims=True)
    leaves[y] = jnp.concatenate([energy[0:2], as_rows([second_energy], 8)[0:6]], axis=0)
    share_leaves = [
        remote(leaves.at[y], leaves.at[y], leaf_send.at[k], leaf_recv.at[k], me ^ (NC * k), expert)
        for k in (2, 1, 3)
    ]
    for c in share_leaves:
        c.start()

    def side_sum(rnd, energy):
        side[rnd, 0] = energy
        copies = [
            remote(side.at[rnd, 0], side.at[rnd, k], side_send.at[rnd, k], side_recv.at[rnd, k], me ^ k, expert)
            for k in range(1, SIDE)
        ]
        for c in copies:
            c.start()
        for c in copies:
            c.wait()
        return jnp.sum(side[rnd], axis=0)

    def plane_share(rnd, energy):
        plane[rnd, 0] = energy
        copies = [
            remote(plane.at[rnd, 0], plane.at[rnd, k], plane_send.at[rnd, k], plane_recv.at[rnd, k], me ^ k, expert)
            for k in OUTWARD
        ]
        for c in copies:
            c.start()
        for c in copies:
            c.wait()

    groups, each, slot_count = feats.shape
    seqs = leaf_mix.shape[0]
    label = lax.broadcasted_iota(jnp.int32, (seqs, slot_count), 0).astype(F32)

    def leaf(g):
        belongs = codes[g, 0:1] == label
        here = feats[g]
        spread = jnp.concatenate(
            [jnp.where(belongs, here[i : i + 1], 0.0).astype(BF16) for i in range(each)], axis=0
        )
        per_seq = jnp.dot(spread, grads[g], preferred_element_type=F32).astype(BF16)
        for h in range(each // 2):
            pair = jnp.concatenate([per_seq[(2 * h + b) * seqs : (2 * h + b + 1) * seqs] for b in range(2)], axis=1)
            mixed = jnp.dot(leaf_mix[...], pair, preferred_element_type=F32)
            nodes[pl.ds(pl.multiple_of(g * 128, 128), 128), h * 256 : (h + 1) * 256] = mixed.astype(BF16)

    for h in range(NC):
        leaf(chip + h)
    for c in pass_grads:
        c.wait()
    for c in share_feats:
        c.wait()
    for by in (1, 3, 2):
        for h in range(NC):
            leaf(turn(y, by) * NC + h)
    source, target, count = nodes, nodes_b, groups
    for c in share_leaves:
        c.wait()
    factor = factors(jnp.concatenate([leaves[n, 0:NC] for n in range(NY)], axis=0))
    for level in range(3):
        sums = []
        for m in range(count // 2):
            weight = jnp.concatenate([factor[2 * m : 2 * m + 1], factor[2 * m + 1 : 2 * m + 2]], axis=1)
            weight = (merge_mix[...].astype(F32) * weight).astype(BF16)
            total = jnp.zeros((128, 128), F32)
            for h in range(NX):
                columns = slice(h * 256, (h + 1) * 256)
                mixed = jnp.dot(weight, source[m * 256 : (m + 1) * 256, columns], preferred_element_type=F32)
                target[m * 128 : (m + 1) * 128, columns] = mixed.astype(BF16)
                total += mixed[:, :128] * mixed[:, :128] + mixed[:, 128:] * mixed[:, 128:]
            sums.append(jnp.sum(total, axis=1, keepdims=True))
        source, target, count = target, source, count // 2
        if level == 0:
            factor = factors(jnp.concatenate([leaves[n, NC : NC + 1] for n in range(NY)], axis=0))
        if level == 1:
            factor = factors(side_sum(0, as_rows(sums, 8)))

    for h in range(NX):
        lines[h] = source[0:128, h * 256 : (h + 1) * 256]
    shares = [
        remote(lines.at[x ^ k], corner.at[k], line_send.at[k], line_recv.at[k], me ^ (SIDE * k), expert)
        for k in range(1, NX)
    ]
    for c in shares:
        c.start()
    corner[0] = lines[x]
    energy = as_rows(sums, 8)
    plane_share(0, jnp.concatenate([energy[0:1], energy[0:1]], axis=1))
    for k in range(NX):
        rows[k] = factors(jnp.sum(plane[0, k * SIDE : (k + 1) * SIDE], axis=0)[:, :128])
    for c in shares:
        c.wait()
    sums = []
    for m in range(2):
        low, high = x ^ (2 * m), x ^ (2 * m + 1)
        weight = jnp.concatenate([rows[low], rows[high]], axis=1)
        weight = (merge_mix[...].astype(F32) * weight).astype(BF16)
        stacked = jnp.concatenate([corner[low], corner[high]], axis=0)
        mixed = jnp.dot(weight, stacked, preferred_element_type=F32)
        corner_b[m * 128 : (m + 1) * 128] = mixed.astype(BF16)
        sums.append(jnp.sum(mixed * mixed, axis=1, keepdims=True))
    energy = as_rows(sums, 8)
    plane_share(1, jnp.concatenate([energy[0:1], energy[1:2]], axis=1))
    energy = jnp.sum(plane[1], axis=0)
    weight = jnp.concatenate([factors(energy[:, :128]), factors(energy[:, 128:])], axis=1)
    weight = (merge_mix[...].astype(F32) * weight).astype(BF16)
    mixed = jnp.dot(weight, corner_b[...], preferred_element_type=F32)
    energy = as_rows([jnp.sum(mixed * mixed, axis=1, keepdims=True)], 8)
    plane_share(2, jnp.concatenate([energy[0:1], energy[0:1]], axis=1))
    factor = factors(jnp.sum(plane[2], axis=0)[:, :128])
    factor = jnp.broadcast_to(factor, (128, 128)).T
    out[...] = (mixed * jnp.concatenate([factor, factor], axis=1)).astype(BF16)


def shards(tokens, routes, lengths, hidden_grad, proj_in, proj_out, leaf_mix, merge_mix):
    tok_dev, width = tokens.shape
    capacity, depth = hidden_grad.shape[3:]
    slot_count = NZ * capacity
    kin, kout = proj_in.shape[2], proj_out.shape[2]
    hbm = pl.BlockSpec(memory_space=pltpu.HBM)
    vmem = pl.BlockSpec(memory_space=pltpu.VMEM)
    dma = pltpu.SemaphoreType.DMA
    columns = kin * kout // SIDE
    result = pl.pallas_call(
        kernel,
        out_shape=jax.ShapeDtypeStruct((128, columns // NX), BF16),
        in_specs=[hbm] * 8,
        out_specs=vmem,
        scratch_shapes=[
            pltpu.VMEM((2, NZ * tok_dev), jnp.int32),
            pltpu.VMEM((1, tok_dev), jnp.int32),
            pltpu.VMEM((128, 128), BF16),
            pltpu.VMEM((128, 256), BF16),
            pltpu.VMEM((NC * tok_dev, width), BF16),
            pltpu.VMEM((kin, width), BF16),
            pltpu.VMEM((4, kin // NC, width), BF16),
            pltpu.VMEM((NX, NY, len(FAR) * kin // NC, width // (NX * NY)), BF16),
            pltpu.VMEM((CHUNKS, slot_count, depth // CHUNKS), BF16),
            pltpu.VMEM((CHUNKS, depth // CHUNKS, kout), BF16),
            pltpu.VMEM((NC * tok_dev, 384), F32),
            pltpu.VMEM((NC, NZ, tok_dev), F32),
            pltpu.VMEM((SIDE, 8, slot_count), F32),
            pltpu.VMEM((SIDE, slot_count, kout), BF16),
            pltpu.VMEM((NZ, pl.cdiv(capacity, 32) * 16, 128), BF16),
            pltpu.VMEM((NC, NZ, pl.cdiv(capacity, 32) * 16, 128), BF16),
            pltpu.VMEM((slot_count, kout), F32),
            pltpu.VMEM((NY, NC, 8, slot_count), F32),
            pltpu.VMEM((SIDE, 8, slot_count), F32),
            pltpu.VMEM((NC, NC, slot_count, slot_count), F32),
            pltpu.VMEM((NC, NC, slot_count, slot_count), BF16),
            pltpu.VMEM((NC, 128, slot_count), BF16),
            pltpu.VMEM((NY, 8, 128), F32),
            pltpu.VMEM((SIDE * 128, columns), BF16),
            pltpu.VMEM((SIDE * 64, columns), BF16),
            pltpu.VMEM((NX, 128, columns // NX), BF16),
            pltpu.VMEM((NX, 128, columns // NX), BF16),
            pltpu.VMEM((256, columns // NX), BF16),
            pltpu.VMEM((1, SIDE, 8, 128), F32),
            pltpu.VMEM((3, PLANE, 1, 256), F32),
            pltpu.VMEM((NX, 1, 128), F32),
            dma((6 + 2 * CHUNKS,)),
            dma((2,)),
            dma((2,)),
            dma((SIDE,)), dma((SIDE,)),
            dma((NY,)), dma((NY,)),
            dma((NY,)), dma((NY,)),
            dma((NZ,)), dma((NZ,)),
            dma((3,)), dma((3,)),
            dma((6 * HOPS,)), dma((6 * HOPS,)),
            dma((NC, NZ)), dma((NC, NZ)),
            dma((NY,)), dma((NY,)),
            dma((NY,)), dma((NY,)),
            dma((1, SIDE)), dma((1, SIDE)),
            dma((3, PLANE)), dma((3, PLANE)),
            dma((NX,)), dma((NX,)),
        ],
        compiler_params=pltpu.CompilerParams(
            collective_id=0, has_side_effects=True, vmem_limit_bytes=58 << 20
        ),
    )(
        tokens, routes.T, lengths[None], hidden_grad.reshape(slot_count, depth), proj_in[0].T, proj_out[0],
        leaf_mix, merge_mix,
    )
    return result[None]


def solution(mesh):
    in_specs = (
        P(("dp", "expert"), None),
        P("dp", None),
        P("dp"),
        P("dp", "expert", None, None, None),
        P("expert", None, None),
        P("expert", None, None),
        P(),
        P(),
    )
    out_specs = P("expert", None, "dp")
    return jax.shard_map(shards, mesh=mesh, in_specs=in_specs, out_specs=out_specs, check_vma=False)
```

```python
import jax
import jax.numpy as jnp
from jax import lax
from jax.experimental import pallas as pl
from jax.experimental.pallas import tpu as pltpu
from jax.sharding import PartitionSpec as P

SEQ_LEN = 8
EPSILON = 1e-06
MESH = pl.DeviceIdType.MESH
NX, NY, NC, NZ = 4, 4, 2, 8
SIDE = NY * NC
PLANE = NX * SIDE
CHUNKS = 8
HOPS = 20
DISTANCE = (0, 1, 2, 1)
OUTWARD = sorted(range(1, PLANE), key=lambda k: (-DISTANCE[k // SIDE] - DISTANCE[k // NC % NY], -k))
FAR = (2, 6, 3, 5, 4)
PIECES = ((0, 1), (2, 3, 4))
BATCHES = ((0, 32, 16), (64, 48, 32))
F32 = jnp.float32
BF16 = jnp.bfloat16


def factors(energy):
    threshold = jnp.mean(energy, axis=-1, keepdims=True)
    return energy / (energy + threshold + EPSILON)


def remote(src, dst, send, recv, dp, expert):
    return pltpu.make_async_remote_copy(
        src_ref=src, dst_ref=dst, send_sem=send, recv_sem=recv,
        device_id={"dp": dp, "expert": expert}, device_id_type=MESH,
    )


def settle(copies):
    for c in copies:
        c.wait_send()
    for c in copies:
        c.wait_recv()


def as_rows(column_sums, count):
    lane = lax.broadcasted_iota(jnp.int32, (128, 128), 1)
    square = jnp.zeros((128, 128), F32)
    for n, sums in enumerate(column_sums):
        square = jnp.where(lane == n, sums, square)
    return square.T[:count]


def kernel(
    tokens, routes_in, lengths_in, hidden, proj_in, proj_out, leaf_in, merge_in, out,
    routes, lengths, leaf_mix, merge_mix,
    both, raw, direct, weights, grad_in, grad_mix, feature, places, codes, grads, sent, got, total, turned, feats,
    gram, products, mixes, leaves,
    nodes, nodes_b, lines, corner, corner_b, side, plane, rows,
    local, token_sem, place_sem, code_send, code_recv, grad_send, grad_recv, pass_send, pass_recv,
    piece_send, piece_recv, direct_send, direct_recv, ring_send, ring_recv, slot_send, slot_recv, feat_send, feat_recv,
    leaf_send, leaf_recv,
    side_send, side_recv, plane_send, plane_recv, line_send, line_recv,
):
    me, expert = lax.axis_index("dp"), lax.axis_index("expert")
    x, y, core = me // SIDE, (me // NC) % NY, me % NC
    pair = me ^ 1
    n_expert = NZ
    tok_dev = tokens.shape[0]
    depth = tokens.shape[1] // (NX * NY)
    capacity = total.shape[0] // NZ
    slot_count = n_expert * capacity
    half_kin = direct.shape[1]

    barrier = pltpu.get_barrier_semaphore()
    peers = [me ^ k for k in range(1, PLANE)]
    for peer in peers:
        pl.semaphore_signal(barrier, inc=1, device_id={"dp": peer, "expert": expert}, device_id_type=MESH)
    for k in range(1, NZ):
        for to in (me, pair):
            pl.semaphore_signal(barrier, inc=1, device_id={"dp": to, "expert": expert ^ k}, device_id_type=MESH)

    load_proj = pltpu.make_async_copy(proj_in, raw, local.at[0])
    load_proj.start()
    small = [
        pltpu.make_async_copy(a, b, local.at[2 + 2 * CHUNKS + n])
        for n, (a, b) in enumerate(
            ((routes_in, routes), (lengths_in, lengths), (leaf_in, leaf_mix), (merge_in, merge_mix))
        )
    ]
    for c in small:
        c.start()
    own_rows = pl.ds(pl.multiple_of(core * tok_dev, tok_dev), tok_dev)
    load_tokens = pltpu.make_async_copy(tokens, both.at[own_rows], local.at[1])
    chunk = hidden.shape[1] // CHUNKS
    loads = []
    for n in range(CHUNKS):
        part = slice(n * chunk, (n + 1) * chunk)
        loads.append((
            pltpu.make_async_copy(hidden.at[:, part], grad_in.at[n], local.at[2 + 2 * n]),
            pltpu.make_async_copy(proj_out.at[part], grad_mix.at[n], local.at[3 + 2 * n]),
        ))
    for pair_of_loads in loads:
        for c in pair_of_loads:
            c.start()
    load_tokens.start()

    load_proj.wait()
    r = lax.broadcasted_iota(jnp.int32, (half_kin, 2 * half_kin), 0)
    c = lax.broadcasted_iota(jnp.int32, (half_kin, 2 * half_kin), 1)
    wanted = (r % 8) // 2 * 16 + r // 8 * 4 + core * 2 + r % 2
    pick = (wanted == c).astype(BF16)
    for n in range(NX):
        part = slice(n * NY * depth, (n + 1) * NY * depth)
        direct[0, :, part] = jnp.dot(pick, raw[:, part], preferred_element_type=F32).astype(BF16)
    direct[3] = jnp.zeros_like(direct[3])
    pl.semaphore_wait(barrier, len(peers) + NC * (NZ - 1))

    spot = pl.ds(pl.multiple_of((x * NY + y) * depth, 128), depth)
    pieces = [
        remote(
            direct.at[0, :, spot], weights.at[x, y, n * half_kin : (n + 1) * half_kin],
            piece_send.at[n], piece_recv.at[n], me, (expert + NZ - away) % NZ,
        )
        for n, away in enumerate(FAR)
    ]
    for n in (4, 2, 3, 0, 1):
        pieces[n].start()
    share_tokens = remote(tokens, both.at[own_rows], token_sem.at[0], token_sem.at[1], pair, expert)
    share_tokens.start()

    for c in small:
        c.wait()
    r = lax.broadcasted_iota(jnp.int32, (tok_dev, tok_dev), 0)
    c = lax.broadcasted_iota(jnp.int32, (tok_dev, tok_dev), 1)
    earlier = (r < c).astype(BF16)
    seq_dev = tok_dev // SEQ_LEN
    lasting = jnp.broadcast_to(lengths[...], (8, tok_dev)).astype(F32).astype(BF16)
    owner = (r == expert * seq_dev + c // SEQ_LEN).astype(BF16)
    lasting = jnp.dot(lasting, owner, preferred_element_type=F32)
    r = lax.broadcasted_iota(jnp.int32, (8, tok_dev), 0)
    c = lax.broadcasted_iota(jnp.int32, (8, tok_dev), 1)
    live = (c % SEQ_LEN).astype(F32) < lasting

    def placed(match):
        before = jnp.dot(match.astype(F32).astype(BF16), earlier, preferred_element_type=F32)
        return jnp.where(match, before, -1.0)

    here = pl.ds(pl.multiple_of(expert * tok_dev, tok_dev), tok_dev)
    match = (routes[0:1, here] == r) | (routes[1:2, here] == r)
    places[core] = jnp.where(live, placed(match), -1.0)
    share_places = remote(places.at[core], places.at[core], place_sem.at[0], place_sem.at[1], pair, expert)
    share_places.start()
    first = jnp.concatenate([routes[0:1, j * tok_dev : (j + 1) * tok_dev] for j in range(n_expert)], axis=0)
    second = jnp.concatenate([routes[1:2, j * tok_dev : (j + 1) * tok_dev] for j in range(n_expert)], axis=0)
    place = placed((first == expert) | (second == expert))
    cell = lax.broadcasted_iota(jnp.int32, (capacity, tok_dev), 0).astype(F32)
    few = capacity // 2
    halves = [slice(s * few, (s + 1) * few) for s in range(2)]
    held = jnp.concatenate(
        [(place[j : j + 1] == cell[rows_of]).astype(F32) for rows_of in halves for j in range(n_expert)], axis=0
    ).astype(BF16)
    number = (c // SEQ_LEN).astype(F32).astype(BF16)
    code = lax.dot_general(number, held, (((1,), (1,)), ((), ())), preferred_element_type=F32)
    source = lax.broadcasted_iota(jnp.int32, (8, slot_count), 1) // few % n_expert
    group = me % SIDE
    codes[group] = code + (source * seq_dev).astype(F32)
    share_codes = [
        remote(codes.at[group], codes.at[group], code_send.at[k], code_recv.at[k], me ^ k, expert)
        for k in range(1, SIDE)
    ]
    for c in share_codes:
        c.start()

    def hop(t, h, source, part, target, n):
        _, half, split = BATCHES[t]
        start, size = ((0, half), (0, split), (split, half - split))[part]
        start += BATCHES[t][0] + h * half
        at_x, at_y = source if h == 0 else source[::-1]
        to_x, to_y = target if h == 0 else target[::-1]
        view = weights.at[at_x, at_y, pl.ds(start, size)]
        n += (2 * t + h) * HOPS
        hops[n] = remote(view, view, ring_send.at[n], ring_recv.at[n], to_x * SIDE + to_y * NC + core, expert)
        hops[n].start()

    hops = {}
    spots = [(x, y), (y, x)]
    turn = lambda v, by: (v + by) % 4

    def first(t, h):
        a, b = spots[h]
        for n, by in enumerate((2, 1, 3)):
            hop(t, h, (a, b), 0, (turn(a, by), b), n)

    def first_on(t, h):
        hops[(2 * t + h) * HOPS + 1].wait_recv()
        hops[(2 * t + h) * HOPS + 2].wait_recv()

    def second(t, h, by):
        a, b = spots[h]
        hop(t, h, (turn(a, by), b), 0, (a, turn(b, 1)), 4 + 4 * by)
        hop(t, h, (turn(a, by), b), 0, (a, turn(b, 3)), 5 + 4 * by)

    def second_on(t, h, by):
        a, b = spots[h]
        n = 4 + 4 * by
        hops[(2 * t + h) * HOPS + n].wait_recv()
        hop(t, h, (turn(a, by), turn(b, 3)), 1, (a, turn(b, 1)), n + 2)
        hops[(2 * t + h) * HOPS + n + 1].wait_recv()
        hop(t, h, (turn(a, by), turn(b, 1)), 2, (a, turn(b, 3)), n + 3)

    def begin(t):
        if t >= len(BATCHES):
            return
        for n in PIECES[t]:
            pieces[n].wait()
        for h in range(2):
            first(t, h)
        for h in range(2):
            second(t, h, 0)

    def go_on(t, step):
        if t >= len(BATCHES):
            return
        for h in range(2):
            if step == 0:
                first_on(t, h)
                second(t, h, 3)
                second(t, h, 1)
            if step == 1:
                hops[(2 * t + h) * HOPS].wait_recv()
                second(t, h, 2)
        for by in ((0,), (3, 1), (2,))[step]:
            for h in range(2):
                second_on(t, h, by)

    def gradients(n):
        for c in loads[n]:
            c.wait()
        product = jnp.dot(grad_in[n], grad_mix[n], preferred_element_type=F32)
        total[...] = product + total[...] if n else product

    begin(0)
    begin(1)
    next_to = [
        remote(
            direct.at[0], direct.at[slot], direct_send.at[slot], direct_recv.at[slot], me, (expert + by) % NZ
        )
        for slot, by in ((1, NZ - 1), (2, 1))
    ]
    for c in next_to:
        c.start()
    gradients(0)
    gradients(1)
    go_on(0, 0)
    begin(2)
    gradients(2)
    gradients(3)
    go_on(1, 0)
    gradients(4)
    go_on(0, 1)
    gradients(5)
    gradients(6)
    go_on(2, 0)
    gradients(7)
    grads[group] = jnp.concatenate(
        [total[j * capacity + s * few : j * capacity + (s + 1) * few] for s in range(2) for j in range(n_expert)], axis=0
    ).astype(BF16)
    share_pair = remote(grads.at[group], grads.at[group], grad_send.at[0], grad_recv.at[0], pair, expert)
    share_pair.start()
    go_on(1, 1)
    go_on(0, 2)
    share_places.wait()
    for c in share_codes:
        c.wait()
    share_pair.wait()
    chip = group - core
    for h in range(NC):
        label = lax.broadcasted_iota(jnp.int32, (128, slot_count), 0).astype(F32)
        belongs = (codes[chip + h, 0:1] == label).astype(F32).astype(BF16)
        mixes[h] = jnp.dot(leaf_mix[...], belongs, preferred_element_type=F32).astype(BF16)
    go_on(2, 1)
    for h in range(NC):
        for b in range(NC):
            gram[h, b] = lax.dot_general(
                grads[chip + h], grads[chip + b], (((1,), (1,)), ((), ())), preferred_element_type=F32
            )
    go_on(1, 2)
    go_on(2, 2)
    load_tokens.wait()
    share_tokens.wait()
    for c in next_to:
        c.wait()
    feature[...] = jnp.zeros_like(feature)
    near = NC * tok_dev // 2
    for n in range(NX * NY):
        part = slice(n * depth, (n + 1) * depth)
        feature[:, :near] += lax.dot_general(
            both[:, part], direct[:, :, part].reshape(near, depth),
            (((1,), (1,)), ((), ())), preferred_element_type=F32,
        )
    def far(by_x, by_y):
        at_x, at_y = turn(x, by_x), turn(y, by_y)
        part = pl.ds(pl.multiple_of((at_x * NY + at_y) * depth, 128), depth)
        feature[:, near : near + weights.shape[2]] += lax.dot_general(
            both[:, part], weights[at_x, at_y], (((1,), (1,)), ((), ())), preferred_element_type=F32
        )

    for by_x in (0, 1, 3):
        for by_y in (0, 1, 3):
            far(by_x, by_y)
    for t in range(len(BATCHES)):
        for h in range(2):
            for by in range(4):
                for n in (2, 3):
                    hops[(2 * t + h) * HOPS + 4 + 4 * by + n].wait_recv()
    for c in hops.values():
        c.wait_send()
    share_grads = [
        remote(grads.at[group], grads.at[group], grad_send.at[k], grad_recv.at[k], me ^ (NC * k), expert)
        for k in range(1, NY)
    ]
    for c in share_grads:
        c.start()

    for by in (0, 1, 3):
        far(2, by)
        far(by, 2)
    far(2, 2)
    order = (0, 1, NZ - 1) + FAR
    bases = [n * half_kin for n in range(3)] + [near + n * half_kin for n in range(len(FAR))]
    block = lax.broadcasted_iota(jnp.int32, (few, 128), 1) // half_kin
    slots = []
    for h in range(NC):
        chosen = jnp.concatenate(
            [(places[h, pl.ds((expert + by) % NZ, 1)] == cell).astype(F32).astype(BF16) for by in order], axis=0
        )
        slots.append(
            jnp.dot(chosen, feature[h * tok_dev : (h + 1) * tok_dev].astype(BF16), preferred_element_type=F32)
        )
    for n, base in enumerate(bases):
        lanes = base // 128 * 128
        tile = jnp.zeros((few, 128), F32)
        for h in range(NC):
            for s in range(2):
                at = n * capacity + s * few
                there = 2 * h + s
                piece = slots[h][at : at + few, lanes : lanes + 128]
                shift = (there * half_kin - base) % 128
                tile = jnp.where(block == there, pltpu.roll(piece, shift, 1) if shift else piece, tile)
        sent[n] = jnp.concatenate([tile, jnp.zeros((sent.shape[1] - few, 128), F32)], axis=0).astype(BF16)
    share_slots = [
        remote(
            sent.at[n], got.at[core, expert], slot_send.at[to, n], slot_recv.at[to, n], pair if to else me,
            (expert + by) % NZ,
        )
        for n, by in reversed(list(enumerate(order))) for to in range(NC) if n or to
    ]
    for c in share_slots:
        c.start()
    got[core, expert] = sent[0]
    pass_grads = []
    for k in range(1, NY):
        share_grads[k - 1].wait()
        far = group ^ (NC * k)
        c = remote(grads.at[far], grads.at[far], pass_send.at[k], pass_recv.at[k], pair, expert)
        c.start()
        pass_grads.append(c)
    settle(share_slots)
    r = lax.broadcasted_iota(jnp.int32, (half_kin, 128), 0)
    c = lax.broadcasted_iota(jnp.int32, (half_kin, 128), 1)
    pick = (c == r).astype(BF16)
    mine = [[], []]
    for to in range(NC):
        whose = core ^ to
        packed = jnp.concatenate([got[whose, j].astype(F32)[:few] for j in range(n_expert)], axis=0)
        for h in range(NC):
            everything = jnp.concatenate(
                [packed if h + s == 0 else pltpu.roll(packed, 128 - (2 * h + s) * half_kin, 1) for s in range(2)],
                axis=0,
            ).astype(BF16)
            lines_of = lax.dot_general(pick, everything, (((1,), (1,)), ((), ())), preferred_element_type=F32)
            mine[h].append(lines_of.astype(BF16))
            if to == 0:
                for there in range(NY):
                    turned[there, h] = lines_of[there * 8 : (there + 1) * 8]
        if to == 0:
            share_feats = [
                remote(
                    turned.at[y ^ k], feats.at[pl.ds(NC * y, NC)], feat_send.at[k], feat_recv.at[k], me ^ (NC * k), expert
                )
                for k in range(1, NY)
            ]
            for c in share_feats:
                c.start()
    feats[pl.ds(NC * y, NC)] = turned[y]

    full = [jnp.concatenate(mine[h], axis=0) for h in range(NC)]
    for h in range(NC):
        for b in range(NC):
            alike = lax.dot_general(full[h], full[b], (((0,), (0,)), ((), ())), preferred_element_type=F32)
            products[h, b] = (alike * gram[h, b]).astype(BF16)
    sums = []
    for h in range(NC):
        mixed = jnp.dot(mixes[h], products[h, h], preferred_element_type=F32)
        sums.append(jnp.sum(mixed * mixes[h].astype(F32), axis=1, keepdims=True))
    energy = as_rows(sums, 8)
    factor = factors(energy)
    weight = jnp.concatenate([factor[0:1], factor[1:2]], axis=1)
    weight = (merge_mix[...].astype(F32) * weight).astype(BF16)
    reach = [
        jnp.dot(weight[:, h * 128 : (h + 1) * 128], mixes[h], preferred_element_type=F32).astype(BF16)
        for h in range(NC)
    ]
    second_energy = jnp.zeros((128, 1), F32)
    for b in range(NC):
        mixed = jnp.dot(reach[0], products[0, b], preferred_element_type=F32)
        mixed += jnp.dot(reach[1], products[1, b], preferred_element_type=F32)
        second_energy += jnp.sum(mixed * reach[b].astype(F32), axis=1, keepdims=True)
    leaves[y] = jnp.concatenate([energy[0:2], as_rows([second_energy], 8)[0:6]], axis=0)
    share_leaves = [
        remote(leaves.at[y], leaves.at[y], leaf_send.at[k], leaf_recv.at[k], me ^ (NC * k), expert)
        for k in (2, 1, 3)
    ]
    for c in share_leaves:
        c.start()

    def side_sum(rnd, energy):
        side[rnd, 0] = energy
        copies = [
            remote(side.at[rnd, 0], side.at[rnd, k], side_send.at[rnd, k], side_recv.at[rnd], me ^ k, expert)
            for k in range(1, SIDE)
        ]
        for c in copies:
            c.start()
        for c in copies:
            c.wait_send()
        pltpu.make_async_copy(side.at[rnd, 1:], side.at[rnd, 1:], side_recv.at[rnd]).wait()
        return jnp.sum(side[rnd], axis=0)

    def plane_share(rnd, energy):
        plane[rnd, 0] = energy
        copies = [
            remote(plane.at[rnd, 0], plane.at[rnd, k], plane_send.at[rnd, k], plane_recv.at[rnd], me ^ k, expert)
            for k in OUTWARD
        ]
        for c in copies:
            c.start()
        for c in copies:
            c.wait_send()
        pltpu.make_async_copy(plane.at[rnd, 1:], plane.at[rnd, 1:], plane_recv.at[rnd]).wait()

    groups, each, slot_count = feats.shape
    seqs = leaf_mix.shape[0]
    label = lax.broadcasted_iota(jnp.int32, (seqs, slot_count), 0).astype(F32)

    def leaf(g):
        belongs = codes[g, 0:1] == label
        here = feats[g]
        spread = jnp.concatenate(
            [jnp.where(belongs, here[i : i + 1], 0.0).astype(BF16) for i in range(each)], axis=0
        )
        per_seq = jnp.dot(spread, grads[g], preferred_element_type=F32).astype(BF16)
        for h in range(each // 2):
            pair = jnp.concatenate([per_seq[(2 * h + b) * seqs : (2 * h + b + 1) * seqs] for b in range(2)], axis=1)
            mixed = jnp.dot(leaf_mix[...], pair, preferred_element_type=F32)
            nodes[pl.ds(pl.multiple_of(g * 128, 128), 128), h * 256 : (h + 1) * 256] = mixed.astype(BF16)

    for h in range(NC):
        leaf(chip + h)
    for c in pass_grads:
        c.wait()
    settle(share_feats)
    for by in (1, 3, 2):
        for h in range(NC):
            leaf(turn(y, by) * NC + h)
    source, target, count = nodes, nodes_b, groups
    settle(share_leaves)
    factor = factors(jnp.concatenate([leaves[n, 0:NC] for n in range(NY)], axis=0))
    for level in range(3):
        sums = []
        for m in range(count // 2):
            weight = jnp.concatenate([factor[2 * m : 2 * m + 1], factor[2 * m + 1 : 2 * m + 2]], axis=1)
            weight = (merge_mix[...].astype(F32) * weight).astype(BF16)
            total = jnp.zeros((128, 128), F32)
            for h in range(NX):
                columns = slice(h * 256, (h + 1) * 256)
                mixed = jnp.dot(weight, source[m * 256 : (m + 1) * 256, columns], preferred_element_type=F32)
                target[m * 128 : (m + 1) * 128, columns] = mixed.astype(BF16)
                total += mixed[:, :128] * mixed[:, :128] + mixed[:, 128:] * mixed[:, 128:]
            sums.append(jnp.sum(total, axis=1, keepdims=True))
        source, target, count = target, source, count // 2
        if level == 0:
            factor = factors(jnp.concatenate([leaves[n, NC : NC + 1] for n in range(NY)], axis=0))
        if level == 1:
            factor = factors(side_sum(0, as_rows(sums, 8)))

    for h in range(NX):
        lines[h] = source[0:128, h * 256 : (h + 1) * 256]
    shares = [
        remote(lines.at[x ^ k], corner.at[k], line_send.at[k], line_recv.at[k], me ^ (SIDE * k), expert)
        for k in range(1, NX)
    ]
    for c in shares:
        c.start()
    corner[0] = lines[x]
    energy = as_rows(sums, 8)
    plane_share(0, jnp.concatenate([energy[0:1], energy[0:1]], axis=1))
    for k in range(NX):
        rows[k] = factors(jnp.sum(plane[0, k * SIDE : (k + 1) * SIDE], axis=0)[:, :128])
    settle(shares)
    sums = []
    for m in range(2):
        low, high = x ^ (2 * m), x ^ (2 * m + 1)
        weight = jnp.concatenate([rows[low], rows[high]], axis=1)
        weight = (merge_mix[...].astype(F32) * weight).astype(BF16)
        stacked = jnp.concatenate([corner[low], corner[high]], axis=0)
        mixed = jnp.dot(weight, stacked, preferred_element_type=F32)
        corner_b[m * 128 : (m + 1) * 128] = mixed.astype(BF16)
        sums.append(jnp.sum(mixed * mixed, axis=1, keepdims=True))
    energy = as_rows(sums, 8)
    plane_share(1, jnp.concatenate([energy[0:1], energy[1:2]], axis=1))
    energy = jnp.sum(plane[1], axis=0)
    weight = jnp.concatenate([factors(energy[:, :128]), factors(energy[:, 128:])], axis=1)
    weight = (merge_mix[...].astype(F32) * weight).astype(BF16)
    mixed = jnp.dot(weight, corner_b[...], preferred_element_type=F32)
    energy = as_rows([jnp.sum(mixed * mixed, axis=1, keepdims=True)], 8)
    plane_share(2, jnp.concatenate([energy[0:1], energy[0:1]], axis=1))
    factor = factors(jnp.sum(plane[2], axis=0)[:, :128])
    factor = jnp.broadcast_to(factor, (128, 128)).T
    out[...] = (mixed * jnp.concatenate([factor, factor], axis=1)).astype(BF16)


def shards(tokens, routes, lengths, hidden_grad, proj_in, proj_out, leaf_mix, merge_mix):
    tok_dev, width = tokens.shape
    capacity, depth = hidden_grad.shape[3:]
    slot_count = NZ * capacity
    kin, kout = proj_in.shape[2], proj_out.shape[2]
    hbm = pl.BlockSpec(memory_space=pltpu.HBM)
    vmem = pl.BlockSpec(memory_space=pltpu.VMEM)
    dma = pltpu.SemaphoreType.DMA
    columns = kin * kout // SIDE
    result = pl.pallas_call(
        kernel,
        out_shape=jax.ShapeDtypeStruct((128, columns // NX), BF16),
        in_specs=[hbm] * 8,
        out_specs=vmem,
        scratch_shapes=[
            pltpu.VMEM((2, NZ * tok_dev), jnp.int32),
            pltpu.VMEM((1, tok_dev), jnp.int32),
            pltpu.VMEM((128, 128), BF16),
            pltpu.VMEM((128, 256), BF16),
            pltpu.VMEM((NC * tok_dev, width), BF16),
            pltpu.VMEM((kin, width), BF16),
            pltpu.VMEM((4, kin // NC, width), BF16),
            pltpu.VMEM((NX, NY, len(FAR) * kin // NC, width // (NX * NY)), BF16),
            pltpu.VMEM((CHUNKS, slot_count, depth // CHUNKS), BF16),
            pltpu.VMEM((CHUNKS, depth // CHUNKS, kout), BF16),
            pltpu.VMEM((NC * tok_dev, 384), F32),
            pltpu.VMEM((NC, NZ, tok_dev), F32),
            pltpu.VMEM((SIDE, 8, slot_count), F32),
            pltpu.VMEM((SIDE, slot_count, kout), BF16),
            pltpu.VMEM((NZ, pl.cdiv(capacity, 32) * 16, 128), BF16),
            pltpu.VMEM((NC, NZ, pl.cdiv(capacity, 32) * 16, 128), BF16),
            pltpu.VMEM((slot_count, kout), F32),
            pltpu.VMEM((NY, NC, 8, slot_count), F32),
            pltpu.VMEM((SIDE, 8, slot_count), F32),
            pltpu.VMEM((NC, NC, slot_count, slot_count), F32),
            pltpu.VMEM((NC, NC, slot_count, slot_count), BF16),
            pltpu.VMEM((NC, 128, slot_count), BF16),
            pltpu.VMEM((NY, 8, 128), F32),
            pltpu.VMEM((SIDE * 128, columns), BF16),
            pltpu.VMEM((SIDE * 64, columns), BF16),
            pltpu.VMEM((NX, 128, columns // NX), BF16),
            pltpu.VMEM((NX, 128, columns // NX), BF16),
            pltpu.VMEM((256, columns // NX), BF16),
            pltpu.VMEM((1, SIDE, 8, 128), F32),
            pltpu.VMEM((3, PLANE, 1, 256), F32),
            pltpu.VMEM((NX, 1, 128), F32),
            dma((6 + 2 * CHUNKS,)),
            dma((2,)),
            dma((2,)),
            dma((SIDE,)), dma((SIDE,)),
            dma((NY,)), dma((NY,)),
            dma((NY,)), dma((NY,)),
            dma((NZ,)), dma((NZ,)),
            dma((3,)), dma((3,)),
            dma((6 * HOPS,)), dma((6 * HOPS,)),
            dma((NC, NZ)), dma((NC, NZ)),
            dma((NY,)), dma((NY,)),
            dma((NY,)), dma((NY,)),
            dma((1, SIDE)), dma((1,)),
            dma((3, PLANE)), dma((3,)),
            dma((NX,)), dma((NX,)),
        ],
        compiler_params=pltpu.CompilerParams(
            collective_id=0, has_side_effects=True, vmem_limit_bytes=58 << 20
        ),
    )(
        tokens, routes.T, lengths[None], hidden_grad.reshape(slot_count, depth), proj_in[0].T, proj_out[0],
        leaf_mix, merge_mix,
    )
    return result[None]


def solution(mesh):
    in_specs = (
        P(("dp", "expert"), None),
        P("dp", None),
        P("dp"),
        P("dp", "expert", None, None, None),
        P("expert", None, None),
        P("expert", None, None),
        P(),
        P(),
    )
    out_specs = P("expert", None, "dp")
    return jax.shard_map(shards, mesh=mesh, in_specs=in_specs, out_specs=out_specs, check_vma=False)
```

```python
import jax
import jax.numpy as jnp
from jax import lax
from jax.experimental import pallas as pl
from jax.experimental.pallas import tpu as pltpu
from jax.sharding import PartitionSpec as P

SEQ_LEN = 8
EPSILON = 1e-06
MESH = pl.DeviceIdType.MESH
NX, NY, NC, NZ = 4, 4, 2, 8
SIDE = NY * NC
PLANE = NX * SIDE
CHUNKS = 8
HOPS = 20
DISTANCE = (0, 1, 2, 1)
OUTWARD = sorted(range(1, PLANE), key=lambda k: (-DISTANCE[k // SIDE] - DISTANCE[k // NC % NY], -k))
FAR = (2, 6, 3, 5, 4)
PIECES = ((0, 1), (2, 3, 4))
BATCHES = ((0, 32, 16), (64, 48, 32))
F32 = jnp.float32
BF16 = jnp.bfloat16


def factors(energy):
    threshold = jnp.mean(energy, axis=-1, keepdims=True)
    return energy / (energy + threshold + EPSILON)


def remote(src, dst, send, recv, dp, expert):
    return pltpu.make_async_remote_copy(
        src_ref=src, dst_ref=dst, send_sem=send, recv_sem=recv,
        device_id={"dp": dp, "expert": expert}, device_id_type=MESH,
    )


def settle(copies):
    for c in copies:
        c.wait_send()
    for c in copies:
        c.wait_recv()


def as_rows(column_sums, count):
    lane = lax.broadcasted_iota(jnp.int32, (128, 128), 1)
    square = jnp.zeros((128, 128), F32)
    for n, sums in enumerate(column_sums):
        square = jnp.where(lane == n, sums, square)
    return square.T[:count]


def kernel(
    tokens, routes_in, lengths_in, hidden, proj_in, proj_out, leaf_in, merge_in, out,
    routes, lengths, leaf_mix, merge_mix,
    both, raw, direct, weights, grad_in, grad_mix, feature, places, codes, grads, sent, got, total, turned, feats,
    gram, products, mixes, leaves,
    nodes, nodes_b, lines, corner, corner_b, side, plane, rows,
    local, token_sem, place_sem, code_send, code_recv, grad_send, grad_recv, pass_send, pass_recv,
    piece_send, piece_recv, direct_send, direct_recv, ring_send, ring_recv, slot_send, slot_recv, feat_send, feat_recv,
    leaf_send, leaf_recv,
    side_send, side_recv, plane_send, plane_recv, line_send, line_recv,
):
    me, expert = lax.axis_index("dp"), lax.axis_index("expert")
    x, y, core = me // SIDE, (me // NC) % NY, me % NC
    pair = me ^ 1
    n_expert = NZ
    tok_dev = tokens.shape[0]
    depth = tokens.shape[1] // (NX * NY)
    capacity = total.shape[0] // NZ
    slot_count = n_expert * capacity
    half_kin = direct.shape[1]

    barrier = pltpu.get_barrier_semaphore()
    peers = [me ^ k for k in range(1, PLANE)]
    for peer in peers:
        pl.semaphore_signal(barrier, inc=1, device_id={"dp": peer, "expert": expert}, device_id_type=MESH)
    for k in range(1, NZ):
        for to in (me, pair):
            pl.semaphore_signal(barrier, inc=1, device_id={"dp": to, "expert": expert ^ k}, device_id_type=MESH)

    load_proj = pltpu.make_async_copy(proj_in, raw, local.at[0])
    load_proj.start()
    small = [
        pltpu.make_async_copy(a, b, local.at[2 + 2 * CHUNKS + n])
        for n, (a, b) in enumerate(
            ((routes_in, routes), (lengths_in, lengths), (leaf_in, leaf_mix), (merge_in, merge_mix))
        )
    ]
    for c in small:
        c.start()
    own_rows = pl.ds(pl.multiple_of(core * tok_dev, tok_dev), tok_dev)
    load_tokens = pltpu.make_async_copy(tokens, both.at[own_rows], local.at[1])
    chunk = hidden.shape[1] // CHUNKS
    loads = []
    for n in range(CHUNKS):
        part = slice(n * chunk, (n + 1) * chunk)
        loads.append((
            pltpu.make_async_copy(hidden.at[:, part], grad_in.at[n], local.at[2 + 2 * n]),
            pltpu.make_async_copy(proj_out.at[part], grad_mix.at[n], local.at[3 + 2 * n]),
        ))
    for pair_of_loads in loads:
        for c in pair_of_loads:
            c.start()
    load_tokens.start()

    load_proj.wait()
    r = lax.broadcasted_iota(jnp.int32, (half_kin, 2 * half_kin), 0)
    c = lax.broadcasted_iota(jnp.int32, (half_kin, 2 * half_kin), 1)
    wanted = (r % 8) // 2 * 16 + r // 8 * 4 + core * 2 + r % 2
    pick = (wanted == c).astype(BF16)
    for n in range(NX):
        part = slice(n * NY * depth, (n + 1) * NY * depth)
        direct[0, :, part] = jnp.dot(pick, raw[:, part], preferred_element_type=F32).astype(BF16)
    direct[3] = jnp.zeros_like(direct[3])
    pl.semaphore_wait(barrier, len(peers) + NC * (NZ - 1))

    spot = pl.ds(pl.multiple_of((x * NY + y) * depth, 128), depth)
    pieces = [
        remote(
            direct.at[0, :, spot], weights.at[x, y, n * half_kin : (n + 1) * half_kin],
            piece_send.at[n], piece_recv.at[n], me, (expert + NZ - away) % NZ,
        )
        for n, away in enumerate(FAR)
    ]
    for n in (4, 2, 3, 0, 1):
        pieces[n].start()
    share_tokens = remote(tokens, both.at[own_rows], token_sem.at[0], token_sem.at[1], pair, expert)
    share_tokens.start()

    for c in small:
        c.wait()
    r = lax.broadcasted_iota(jnp.int32, (tok_dev, tok_dev), 0)
    c = lax.broadcasted_iota(jnp.int32, (tok_dev, tok_dev), 1)
    earlier = (r < c).astype(BF16)
    seq_dev = tok_dev // SEQ_LEN
    lasting = jnp.broadcast_to(lengths[...], (8, tok_dev)).astype(F32).astype(BF16)
    owner = (r == expert * seq_dev + c // SEQ_LEN).astype(BF16)
    lasting = jnp.dot(lasting, owner, preferred_element_type=F32)
    r = lax.broadcasted_iota(jnp.int32, (8, tok_dev), 0)
    c = lax.broadcasted_iota(jnp.int32, (8, tok_dev), 1)
    live = (c % SEQ_LEN).astype(F32) < lasting

    def placed(match):
        before = jnp.dot(match.astype(F32).astype(BF16), earlier, preferred_element_type=F32)
        return jnp.where(match, before, -1.0)

    here = pl.ds(pl.multiple_of(expert * tok_dev, tok_dev), tok_dev)
    match = (routes[0:1, here] == r) | (routes[1:2, here] == r)
    places[core] = jnp.where(live, placed(match), -1.0)
    share_places = remote(places.at[core], places.at[core], place_sem.at[0], place_sem.at[1], pair, expert)
    share_places.start()
    first = jnp.concatenate([routes[0:1, j * tok_dev : (j + 1) * tok_dev] for j in range(n_expert)], axis=0)
    second = jnp.concatenate([routes[1:2, j * tok_dev : (j + 1) * tok_dev] for j in range(n_expert)], axis=0)
    place = placed((first == expert) | (second == expert))
    cell = lax.broadcasted_iota(jnp.int32, (capacity, tok_dev), 0).astype(F32)
    few = capacity // 2
    halves = [slice(s * few, (s + 1) * few) for s in range(2)]
    held = jnp.concatenate(
        [(place[j : j + 1] == cell[rows_of]).astype(F32) for rows_of in halves for j in range(n_expert)], axis=0
    ).astype(BF16)
    number = (c // SEQ_LEN).astype(F32).astype(BF16)
    code = lax.dot_general(number, held, (((1,), (1,)), ((), ())), preferred_element_type=F32)
    source = lax.broadcasted_iota(jnp.int32, (8, slot_count), 1) // few % n_expert
    group = me % SIDE
    codes[group] = code + (source * seq_dev).astype(F32)
    share_codes = [
        remote(codes.at[group], codes.at[group], code_send.at[k], code_recv.at[k], me ^ k, expert)
        for k in range(1, SIDE)
    ]
    for c in share_codes:
        c.start()

    def hop(t, h, source, part, target, n):
        _, half, split = BATCHES[t]
        start, size = ((0, half), (0, split), (split, half - split))[part]
        start += BATCHES[t][0] + h * half
        at_x, at_y = source if h == 0 else source[::-1]
        to_x, to_y = target if h == 0 else target[::-1]
        view = weights.at[at_x, at_y, pl.ds(start, size)]
        n += (2 * t + h) * HOPS
        hops[n] = remote(view, view, ring_send.at[n], ring_recv.at[n], to_x * SIDE + to_y * NC + core, expert)
        hops[n].start()

    hops = {}
    spots = [(x, y), (y, x)]
    turn = lambda v, by: (v + by) % 4

    def first(t, h):
        a, b = spots[h]
        for n, by in enumerate((2, 1, 3)):
            hop(t, h, (a, b), 0, (turn(a, by), b), n)

    def first_on(t, h):
        hops[(2 * t + h) * HOPS + 1].wait_recv()
        hops[(2 * t + h) * HOPS + 2].wait_recv()

    def second(t, h, by):
        a, b = spots[h]
        hop(t, h, (turn(a, by), b), 0, (a, turn(b, 1)), 4 + 4 * by)
        hop(t, h, (turn(a, by), b), 0, (a, turn(b, 3)), 5 + 4 * by)

    def second_on(t, h, by):
        a, b = spots[h]
        n = 4 + 4 * by
        hops[(2 * t + h) * HOPS + n].wait_recv()
        hop(t, h, (turn(a, by), turn(b, 3)), 1, (a, turn(b, 1)), n + 2)
        hops[(2 * t + h) * HOPS + n + 1].wait_recv()
        hop(t, h, (turn(a, by), turn(b, 1)), 2, (a, turn(b, 3)), n + 3)

    def begin(t):
        if t >= len(BATCHES):
            return
        for n in PIECES[t]:
            pieces[n].wait()
        for h in range(2):
            first(t, h)
        for h in range(2):
            second(t, h, 0)

    def go_on(t, step):
        if t >= len(BATCHES):
            return
        for h in range(2):
            if step == 0:
                first_on(t, h)
                second(t, h, 3)
                second(t, h, 1)
            if step == 1:
                hops[(2 * t + h) * HOPS].wait_recv()
                second(t, h, 2)
        for by in ((0,), (3, 1), (2,))[step]:
            for h in range(2):
                second_on(t, h, by)

    def gradients(n):
        for c in loads[n]:
            c.wait()
        product = jnp.dot(grad_in[n], grad_mix[n], preferred_element_type=F32)
        total[...] = product + total[...] if n else product

    begin(0)
    begin(1)
    next_to = [
        remote(
            direct.at[0], direct.at[slot], direct_send.at[slot], direct_recv.at[slot], me, (expert + by) % NZ
        )
        for slot, by in ((1, NZ - 1), (2, 1))
    ]
    for c in next_to:
        c.start()
    gradients(0)
    gradients(1)
    go_on(0, 0)
    begin(2)
    gradients(2)
    gradients(3)
    go_on(1, 0)
    gradients(4)
    go_on(0, 1)
    gradients(5)
    gradients(6)
    go_on(2, 0)
    gradients(7)
    grads[group] = jnp.concatenate(
        [total[j * capacity + s * few : j * capacity + (s + 1) * few] for s in range(2) for j in range(n_expert)], axis=0
    ).astype(BF16)
    share_pair = remote(grads.at[group], grads.at[group], grad_send.at[0], grad_recv.at[0], pair, expert)
    share_pair.start()
    go_on(1, 1)
    go_on(0, 2)
    share_places.wait()
    for c in share_codes:
        c.wait()
    share_pair.wait()
    chip = group - core
    for h in range(NC):
        label = lax.broadcasted_iota(jnp.int32, (128, slot_count), 0).astype(F32)
        belongs = (codes[chip + h, 0:1] == label).astype(F32).astype(BF16)
        mixes[h] = jnp.dot(leaf_mix[...], belongs, preferred_element_type=F32).astype(BF16)
    go_on(2, 1)
    for h in range(NC):
        for b in range(NC):
            gram[h, b] = lax.dot_general(
                grads[chip + h], grads[chip + b], (((1,), (1,)), ((), ())), preferred_element_type=F32
            )
    go_on(1, 2)
    go_on(2, 2)
    load_tokens.wait()
    share_tokens.wait()
    for c in next_to:
        c.wait()
    feature[...] = jnp.zeros_like(feature)
    near = NC * tok_dev // 2
    for n in range(NX * NY):
        part = slice(n * depth, (n + 1) * depth)
        feature[:, :near] += lax.dot_general(
            both[:, part], direct[:, :, part].reshape(near, depth),
            (((1,), (1,)), ((), ())), preferred_element_type=F32,
        )
    def far(by_x, by_y):
        at_x, at_y = turn(x, by_x), turn(y, by_y)
        part = pl.ds(pl.multiple_of((at_x * NY + at_y) * depth, 128), depth)
        feature[:, near : near + weights.shape[2]] += lax.dot_general(
            both[:, part], weights[at_x, at_y], (((1,), (1,)), ((), ())), preferred_element_type=F32
        )

    for by_x in (0, 1, 3):
        for by_y in (0, 1, 3):
            far(by_x, by_y)
    for t in range(len(BATCHES)):
        for h in range(2):
            for by in range(4):
                for n in (2, 3):
                    hops[(2 * t + h) * HOPS + 4 + 4 * by + n].wait_recv()
    share_grads = [
        remote(grads.at[group], grads.at[group], grad_send.at[k], grad_recv.at[k], me ^ (NC * k), expert)
        for k in range(1, NY)
    ]
    for c in share_grads:
        c.start()

    for by in (0, 1, 3):
        far(2, by)
        far(by, 2)
    far(2, 2)
    order = (0, 1, NZ - 1) + FAR
    bases = [n * half_kin for n in range(3)] + [near + n * half_kin for n in range(len(FAR))]
    block = lax.broadcasted_iota(jnp.int32, (few, 128), 1) // half_kin
    slots = []
    for h in range(NC):
        chosen = jnp.concatenate(
            [(places[h, pl.ds((expert + by) % NZ, 1)] == cell).astype(F32).astype(BF16) for by in order], axis=0
        )
        slots.append(
            jnp.dot(chosen, feature[h * tok_dev : (h + 1) * tok_dev].astype(BF16), preferred_element_type=F32)
        )
    for n, base in enumerate(bases):
        lanes = base // 128 * 128
        tile = jnp.zeros((few, 128), F32)
        for h in range(NC):
            for s in range(2):
                at = n * capacity + s * few
                there = 2 * h + s
                piece = slots[h][at : at + few, lanes : lanes + 128]
                shift = (there * half_kin - base) % 128
                tile = jnp.where(block == there, pltpu.roll(piece, shift, 1) if shift else piece, tile)
        sent[n] = jnp.concatenate([tile, jnp.zeros((sent.shape[1] - few, 128), F32)], axis=0).astype(BF16)
    share_slots = [
        remote(
            sent.at[n], got.at[core, expert], slot_send.at[to, n], slot_recv.at[to, n], pair if to else me,
            (expert + by) % NZ,
        )
        for n, by in reversed(list(enumerate(order))) for to in range(NC) if n or to
    ]
    for c in share_slots:
        c.start()
    got[core, expert] = sent[0]
    for c in hops.values():
        c.wait_send()
    pass_grads = []
    for k in range(1, NY):
        share_grads[k - 1].wait()
        far = group ^ (NC * k)
        c = remote(grads.at[far], grads.at[far], pass_send.at[k], pass_recv.at[k], pair, expert)
        c.start()
        pass_grads.append(c)
    settle(share_slots)
    r = lax.broadcasted_iota(jnp.int32, (half_kin, 128), 0)
    c = lax.broadcasted_iota(jnp.int32, (half_kin, 128), 1)
    pick = (c == r).astype(BF16)
    mine = [[], []]
    for to in range(NC):
        whose = core ^ to
        packed = jnp.concatenate([got[whose, j].astype(F32)[:few] for j in range(n_expert)], axis=0)
        for h in range(NC):
            everything = jnp.concatenate(
                [packed if h + s == 0 else pltpu.roll(packed, 128 - (2 * h + s) * half_kin, 1) for s in range(2)],
                axis=0,
            ).astype(BF16)
            lines_of = lax.dot_general(pick, everything, (((1,), (1,)), ((), ())), preferred_element_type=F32)
            mine[h].append(lines_of.astype(BF16))
            if to == 0:
                for there in range(NY):
                    turned[there, h] = lines_of[there * 8 : (there + 1) * 8]
        if to == 0:
            share_feats = [
                remote(
                    turned.at[y ^ k], feats.at[pl.ds(NC * y, NC)], feat_send.at[k], feat_recv.at[k], me ^ (NC * k), expert
                )
                for k in range(1, NY)
            ]
            for c in share_feats:
                c.start()
    feats[pl.ds(NC * y, NC)] = turned[y]

    full = [jnp.concatenate(mine[h], axis=0) for h in range(NC)]
    for h in range(NC):
        for b in range(NC):
            alike = lax.dot_general(full[h], full[b], (((0,), (0,)), ((), ())), preferred_element_type=F32)
            products[h, b] = (alike * gram[h, b]).astype(BF16)
    sums = []
    for h in range(NC):
        mixed = jnp.dot(mixes[h], products[h, h], preferred_element_type=F32)
        sums.append(jnp.sum(mixed * mixes[h].astype(F32), axis=1, keepdims=True))
    energy = as_rows(sums, 8)
    factor = factors(energy)
    weight = jnp.concatenate([factor[0:1], factor[1:2]], axis=1)
    weight = (merge_mix[...].astype(F32) * weight).astype(BF16)
    reach = [
        jnp.dot(weight[:, h * 128 : (h + 1) * 128], mixes[h], preferred_element_type=F32).astype(BF16)
        for h in range(NC)
    ]
    second_energy = jnp.zeros((128, 1), F32)
    for b in range(NC):
        mixed = jnp.dot(reach[0], products[0, b], preferred_element_type=F32)
        mixed += jnp.dot(reach[1], products[1, b], preferred_element_type=F32)
        second_energy += jnp.sum(mixed * reach[b].astype(F32), axis=1, keepdims=True)
    leaves[y] = jnp.concatenate([energy[0:2], as_rows([second_energy], 8)[0:6]], axis=0)
    share_leaves = [
        remote(leaves.at[y], leaves.at[y], leaf_send.at[k], leaf_recv.at[k], me ^ (NC * k), expert)
        for k in (2, 1, 3)
    ]
    for c in share_leaves:
        c.start()

    def side_sum(rnd, energy):
        side[rnd, 0] = energy
        copies = [
            remote(side.at[rnd, 0], side.at[rnd, k], side_send.at[rnd, k], side_recv.at[rnd], me ^ k, expert)
            for k in range(1, SIDE)
        ]
        for c in copies:
            c.start()
        for c in copies:
            c.wait_send()
        pltpu.make_async_copy(side.at[rnd, 1:], side.at[rnd, 1:], side_recv.at[rnd]).wait()
        return jnp.sum(side[rnd], axis=0)

    def plane_share(rnd, energy):
        plane[rnd, 0] = energy
        copies = [
            remote(plane.at[rnd, 0], plane.at[rnd, k], plane_send.at[rnd, k], plane_recv.at[rnd], me ^ k, expert)
            for k in OUTWARD
        ]
        for c in copies:
            c.start()
        for c in copies:
            c.wait_send()
        pltpu.make_async_copy(plane.at[rnd, 1:], plane.at[rnd, 1:], plane_recv.at[rnd]).wait()

    groups, each, slot_count = feats.shape
    seqs = leaf_mix.shape[0]
    label = lax.broadcasted_iota(jnp.int32, (seqs, slot_count), 0).astype(F32)

    def leaf(g):
        belongs = codes[g, 0:1] == label
        here = feats[g]
        spread = jnp.concatenate(
            [jnp.where(belongs, here[i : i + 1], 0.0).astype(BF16) for i in range(each)], axis=0
        )
        per_seq = jnp.dot(spread, grads[g], preferred_element_type=F32).astype(BF16)
        for h in range(each // 2):
            pair = jnp.concatenate([per_seq[(2 * h + b) * seqs : (2 * h + b + 1) * seqs] for b in range(2)], axis=1)
            mixed = jnp.dot(leaf_mix[...], pair, preferred_element_type=F32)
            nodes[pl.ds(pl.multiple_of(g * 128, 128), 128), h * 256 : (h + 1) * 256] = mixed.astype(BF16)

    for h in range(NC):
        leaf(chip + h)
    for c in pass_grads:
        c.wait()
    settle(share_feats)
    for by in (1, 3, 2):
        for h in range(NC):
            leaf(turn(y, by) * NC + h)
    source, target, count = nodes, nodes_b, groups
    settle(share_leaves)
    factor = factors(jnp.concatenate([leaves[n, 0:NC] for n in range(NY)], axis=0))
    for level in range(3):
        sums = []
        for m in range(count // 2):
            weight = jnp.concatenate([factor[2 * m : 2 * m + 1], factor[2 * m + 1 : 2 * m + 2]], axis=1)
            weight = (merge_mix[...].astype(F32) * weight).astype(BF16)
            total = jnp.zeros((128, 128), F32)
            for h in range(NX):
                columns = slice(h * 256, (h + 1) * 256)
                mixed = jnp.dot(weight, source[m * 256 : (m + 1) * 256, columns], preferred_element_type=F32)
                target[m * 128 : (m + 1) * 128, columns] = mixed.astype(BF16)
                total += mixed[:, :128] * mixed[:, :128] + mixed[:, 128:] * mixed[:, 128:]
            sums.append(jnp.sum(total, axis=1, keepdims=True))
        source, target, count = target, source, count // 2
        if level == 0:
            factor = factors(jnp.concatenate([leaves[n, NC : NC + 1] for n in range(NY)], axis=0))
        if level == 1:
            factor = factors(side_sum(0, as_rows(sums, 8)))

    for h in range(NX):
        lines[h] = source[0:128, h * 256 : (h + 1) * 256]
    shares = [
        remote(lines.at[x ^ k], corner.at[k], line_send.at[k], line_recv.at[k], me ^ (SIDE * k), expert)
        for k in range(1, NX)
    ]
    for c in shares:
        c.start()
    corner[0] = lines[x]
    energy = as_rows(sums, 8)
    plane_share(0, jnp.concatenate([energy[0:1], energy[0:1]], axis=1))
    for k in range(NX):
        rows[k] = factors(jnp.sum(plane[0, k * SIDE : (k + 1) * SIDE], axis=0)[:, :128])
    settle(shares)
    sums = []
    for m in range(2):
        low, high = x ^ (2 * m), x ^ (2 * m + 1)
        weight = jnp.concatenate([rows[low], rows[high]], axis=1)
        weight = (merge_mix[...].astype(F32) * weight).astype(BF16)
        stacked = jnp.concatenate([corner[low], corner[high]], axis=0)
        mixed = jnp.dot(weight, stacked, preferred_element_type=F32)
        corner_b[m * 128 : (m + 1) * 128] = mixed.astype(BF16)
        sums.append(jnp.sum(mixed * mixed, axis=1, keepdims=True))
    energy = as_rows(sums, 8)
    plane_share(1, jnp.concatenate([energy[0:1], energy[1:2]], axis=1))
    energy = jnp.sum(plane[1], axis=0)
    weight = jnp.concatenate([factors(energy[:, :128]), factors(energy[:, 128:])], axis=1)
    weight = (merge_mix[...].astype(F32) * weight).astype(BF16)
    mixed = jnp.dot(weight, corner_b[...], preferred_element_type=F32)
    energy = as_rows([jnp.sum(mixed * mixed, axis=1, keepdims=True)], 8)
    plane_share(2, jnp.concatenate([energy[0:1], energy[0:1]], axis=1))
    factor = factors(jnp.sum(plane[2], axis=0)[:, :128])
    factor = jnp.broadcast_to(factor, (128, 128)).T
    out[...] = (mixed * jnp.concatenate([factor, factor], axis=1)).astype(BF16)


def shards(tokens, routes, lengths, hidden_grad, proj_in, proj_out, leaf_mix, merge_mix):
    tok_dev, width = tokens.shape
    capacity, depth = hidden_grad.shape[3:]
    slot_count = NZ * capacity
    kin, kout = proj_in.shape[2], proj_out.shape[2]
    hbm = pl.BlockSpec(memory_space=pltpu.HBM)
    vmem = pl.BlockSpec(memory_space=pltpu.VMEM)
    dma = pltpu.SemaphoreType.DMA
    columns = kin * kout // SIDE
    result = pl.pallas_call(
        kernel,
        out_shape=jax.ShapeDtypeStruct((128, columns // NX), BF16),
        in_specs=[hbm] * 8,
        out_specs=vmem,
        scratch_shapes=[
            pltpu.VMEM((2, NZ * tok_dev), jnp.int32),
            pltpu.VMEM((1, tok_dev), jnp.int32),
            pltpu.VMEM((128, 128), BF16),
            pltpu.VMEM((128, 256), BF16),
            pltpu.VMEM((NC * tok_dev, width), BF16),
            pltpu.VMEM((kin, width), BF16),
            pltpu.VMEM((4, kin // NC, width), BF16),
            pltpu.VMEM((NX, NY, len(FAR) * kin // NC, width // (NX * NY)), BF16),
            pltpu.VMEM((CHUNKS, slot_count, depth // CHUNKS), BF16),
            pltpu.VMEM((CHUNKS, depth // CHUNKS, kout), BF16),
            pltpu.VMEM((NC * tok_dev, 384), F32),
            pltpu.VMEM((NC, NZ, tok_dev), F32),
            pltpu.VMEM((SIDE, 8, slot_count), F32),
            pltpu.VMEM((SIDE, slot_count, kout), BF16),
            pltpu.VMEM((NZ, pl.cdiv(capacity, 32) * 16, 128), BF16),
            pltpu.VMEM((NC, NZ, pl.cdiv(capacity, 32) * 16, 128), BF16),
            pltpu.VMEM((slot_count, kout), F32),
            pltpu.VMEM((NY, NC, 8, slot_count), F32),
            pltpu.VMEM((SIDE, 8, slot_count), F32),
            pltpu.VMEM((NC, NC, slot_count, slot_count), F32),
            pltpu.VMEM((NC, NC, slot_count, slot_count), BF16),
            pltpu.VMEM((NC, 128, slot_count), BF16),
            pltpu.VMEM((NY, 8, 128), F32),
            pltpu.VMEM((SIDE * 128, columns), BF16),
            pltpu.VMEM((SIDE * 64, columns), BF16),
            pltpu.VMEM((NX, 128, columns // NX), BF16),
            pltpu.VMEM((NX, 128, columns // NX), BF16),
            pltpu.VMEM((256, columns // NX), BF16),
            pltpu.VMEM((1, SIDE, 8, 128), F32),
            pltpu.VMEM((3, PLANE, 1, 256), F32),
            pltpu.VMEM((NX, 1, 128), F32),
            dma((6 + 2 * CHUNKS,)),
            dma((2,)),
            dma((2,)),
            dma((SIDE,)), dma((SIDE,)),
            dma((NY,)), dma((NY,)),
            dma((NY,)), dma((NY,)),
            dma((NZ,)), dma((NZ,)),
            dma((3,)), dma((3,)),
            dma((6 * HOPS,)), dma((6 * HOPS,)),
            dma((NC, NZ)), dma((NC, NZ)),
            dma((NY,)), dma((NY,)),
            dma((NY,)), dma((NY,)),
            dma((1, SIDE)), dma((1,)),
            dma((3, PLANE)), dma((3,)),
            dma((NX,)), dma((NX,)),
        ],
        compiler_params=pltpu.CompilerParams(
            collective_id=0, has_side_effects=True, vmem_limit_bytes=58 << 20
        ),
    )(
        tokens, routes.T, lengths[None], hidden_grad.reshape(slot_count, depth), proj_in[0].T, proj_out[0],
        leaf_mix, merge_mix,
    )
    return result[None]


def solution(mesh):
    in_specs = (
        P(("dp", "expert"), None),
        P("dp", None),
        P("dp"),
        P("dp", "expert", None, None, None),
        P("expert", None, None),
        P("expert", None, None),
        P(),
        P(),
    )
    out_specs = P("expert", None, "dp")
    return jax.shard_map(shards, mesh=mesh, in_specs=in_specs, out_specs=out_specs, check_vma=False)
```
